256 devices in a mesh: rep: 8 (over z), exp: 32 (over x, y, core).
Axes of the slice: x: 4, y: 4, z: 8, core: 2. Of those that a mesh axis runs over, the one named last changes fastest.
Arguments:
- tokens: bfloat16 [4096, 4096], P(('rep', 'exp')), may hold values from -6 to 6
- routed_experts: int32 [4096, 8], P(('rep', 'exp')), may hold values from 0 to 63, all different within a row; in each aligned block of 16 rows (0 to 15, 16 to 31, ...) at most 3 rows name the same one
- route_weights: float32 [4096, 8], P(('rep', 'exp')), may hold values from 0.02 to 0.5
- gate_weight: bfloat16 [64, 1536, 4096], P('exp', 'rep'), may hold values from -0.09375 to 0.09375
- up_weight: bfloat16 [64, 1536, 4096], P('exp', 'rep'), may hold values from -0.09375 to 0.09375
- down_weight: bfloat16 [64, 1536, 4096], P('exp', 'rep'), may hold values from -0.15625 to 0.15625
Outputs:
- layer_output: bfloat16 [4096, 4096], P(('rep', 'exp'))
The draws below stay inside these ranges and needn't reach their ends.
Inputs may be any that keep to these rules, and one draw needn't show every extreme that they name: `routed_experts`: each token names 8 different experts. Among the 16 tokens of one device (aligned blocks of rows), no expert is named more than 3 times, a bound that some block reaches.
All inputs are finite; a program needn't handle non-finite values.
Results may differ from the reference program's by a relative error of at most 0.01.
Values may be sent and summed in bfloat16 or wider, within the bound.
A program may use at most 128 MiB of HBM per device.

```python
import math
import jax
import jax.numpy as jnp
import numpy as np
from jax import lax

D = 4096
FF = 1536
TOP = 8
TOK_DEV = 16
EXPERTS = 64
SHARD_FF = 192
CAP = 3
TOKENS = 4096
N_REP = 8
N_EXP = 32


def steps_of(stream_key, dims, cuts, least, top_value):
    def one(position, shards_of):
        heights = jax.random.uniform(jax.random.fold_in(jax.random.fold_in(stream_key, 6), position), (shards_of,), jnp.float32, least / len(cuts), top_value / len(cuts))
        return jnp.repeat(jnp.exp(heights), dims[position] // shards_of).reshape((-1,) + (1,) * (len(dims) - position - 1))

    level = one(*cuts[0])
    for cut in cuts[1:]:
        level = level * one(*cut)
    return level


def assign_block(own_key, own, number, rows, number_of, top, most, skew):
    ranking = jax.random.permutation(own_key, number_of)
    heavy_load, ordinary = shares(number_of, rows * top, most, skew, True), shares(number_of, rows * top, most, skew, False)
    places = jnp.arange(number_of)

    def named(sizes, rotation):
        used = int((sizes > 0).sum())
        fixed = max(1, used // 4)
        passed = fixed + (places - fixed + rotation * (used - fixed)) % max(1, number_of - fixed)
        return jnp.zeros((number_of,), jnp.int32).at[ranking[jnp.where(places < fixed, places, passed)]].set(jnp.asarray(sizes, jnp.int32))

    sizes = jnp.where(number % 4 == 0, named(heavy_load, number // 4), named(ordinary, number - number // 4 - 1))
    mixed = jax.random.permutation(jax.random.fold_in(own, 3), number_of)
    giver, sink = mixed[0:number_of // 2 * 2:2], mixed[1:number_of // 2 * 2:2]
    slack = jnp.minimum(sizes[giver] - 1, most - sizes[sink]) // 2
    slack = jnp.where((giver == ranking[0]) | (sink == ranking[0]) | (sizes[sink] == 0), 0, jnp.maximum(slack, 0))
    passed = jax.random.randint(jax.random.fold_in(own, 4), (number_of // 2,), 0, 1 << 20) % (slack + 1)
    sizes = sizes.at[giver].add(-passed).at[sink].add(passed)
    items = jnp.searchsorted(jnp.cumsum(sizes), jnp.arange(rows * top), side="right").astype(jnp.int32)
    grid = items.reshape(top, rows).T
    grid = grid[jax.random.permutation(jax.random.fold_in(own, 1), rows)]
    rotation = jax.random.randint(jax.random.fold_in(own, 2), (rows, 1), 0, top)
    return jnp.take_along_axis(grid, (jnp.arange(top)[None, :] + rotation) % top, axis=1)


def shares(count, total, most, lean, full):
    loads = [(1 << 20) // math.isqrt(standing ** lean) + 1 for standing in range(1, count + 1)]
    largest = most if full else min(most, max(-(-total // count), total * loads[0] // sum(loads)))
    least = 1 if total - largest >= count - 1 else 0
    counts, rest = [largest] + [least] * (count - 1), total - largest - least * (count - 1)
    while rest > 0:
        candidates = [i for i in range(1, count) if counts[i] < largest] or [i for i in range(1, count) if counts[i] < most]
        whole, remaining = sum([loads[i] for i in candidates]), rest
        for i in candidates:
            extra = min(most - counts[i], max(1, remaining * loads[i] // whole), rest)
            counts[i] = counts[i] + extra
            rest = rest - extra
    return np.array(counts)


def normal_values(key, shape, deviation, most, cuts=(), kind=jnp.bfloat16):
    array = jax.random.normal(key, shape, jnp.float32) * deviation
    if len(cuts) > 0:
        array = steps_of(key, shape, cuts, -0.22, 0.18) * array
    return jnp.clip(array, min=-most, max=most).astype(kind)


def setup_inputs(seed: int = 0) -> dict:
    key_of = jax.random.split(jax.random.key(seed), 7)
    tokens = normal_values(key_of[0], (TOKENS, D), 1.0, 6.0, ((0, 256),))
    routed_experts_keys = jax.random.split(jax.random.fold_in(key_of[1], 1), TOKENS // TOK_DEV)
    routed_experts_turns = jax.random.permutation(jax.random.fold_in(key_of[1], 3), TOKENS // TOK_DEV)
    routed_experts = jax.vmap(lambda own, number: assign_block(jax.random.fold_in(key_of[1], 2), own, number, TOK_DEV, EXPERTS, TOP, CAP, 2))(routed_experts_keys, routed_experts_turns).reshape((TOKENS, TOP))
    route_weights = jnp.clip(jnp.exp(math.log(0.5) - 3.218876 * jax.random.uniform(key_of[2], (TOKENS, TOP), jnp.float32) ** steps_of(key_of[2], (TOKENS, TOP), ((0, 256),), -0.2, 0.2)), 0.02, 0.5)
    gate_weight = normal_values(key_of[3], (EXPERTS, FF, D), D ** -0.5, 0.09375, ((0, 32), (1, 8)))
    up_weight = normal_values(key_of[4], (EXPERTS, FF, D), D ** -0.5, 0.09375, ((0, 32), (1, 8)))
    down_weight = normal_values(key_of[5], (EXPERTS, FF, D), FF ** -0.5, 0.15625, ((0, 32), (1, 8)))
    return {"tokens": tokens, "routed_experts": routed_experts, "route_weights": route_weights, "gate_weight": gate_weight, "up_weight": up_weight, "down_weight": down_weight}


def reference(tokens, routed_experts, route_weights, gate_weight, up_weight, down_weight):
    flat_experts = routed_experts.reshape(-1)
    flat_weights = route_weights.reshape(-1)
    slot_limit = CAP * N_REP * N_EXP

    def one_expert(accumulated, expert):
        chosen = flat_experts == expert
        expert_load = jnp.sum(chosen.astype(jnp.int32))
        indices = jnp.nonzero(chosen, size=slot_limit, fill_value=0)[0].astype(jnp.int32)
        filled = jnp.arange(slot_limit, dtype=jnp.int32) < expert_load
        token_index = (indices // TOP).astype(jnp.int32)
        weight = jnp.where(filled, flat_weights[indices], jnp.float32(0.0))
        token_rows = tokens[token_index]
        gate_expert = gate_weight[expert]
        up_expert = up_weight[expert]
        down_expert = down_weight[expert]
        summed = jnp.zeros((slot_limit, D), jnp.float32)
        for hidden_group in range(N_REP):
            first_unit = hidden_group * SHARD_FF
            last_unit = first_unit + SHARD_FF
            gate_value = jnp.dot(token_rows, gate_expert[first_unit:last_unit].T, preferred_element_type=jnp.float32)
            up_value = jnp.dot(token_rows, up_expert[first_unit:last_unit].T, preferred_element_type=jnp.float32)
            hidden = (jax.nn.silu(gate_value) * up_value).astype(jnp.bfloat16)
            group_part = jnp.dot(hidden, down_expert[first_unit:last_unit], preferred_element_type=jnp.float32)
            group_part = lax.optimization_barrier(group_part.astype(jnp.bfloat16))
            summed = summed + group_part.astype(jnp.float32)
        accumulated = accumulated.at[token_index].add(summed * weight[:, None])
        return accumulated, None

    accumulated, _ = lax.scan(one_expert, jnp.zeros((TOKENS, D), jnp.float32), jnp.arange(EXPERTS, dtype=jnp.int32))
    return accumulated.astype(jnp.bfloat16)
```

```python
import heapq

import jax
import jax.numpy as jnp
from jax import lax
from jax.experimental import pallas as pl
from jax.experimental.pallas import tpu as pltpu
from jax.sharding import PartitionSpec as P

MESH = pl.DeviceIdType.MESH
LANES = 128
CAPACITY = 3
GROUPS_PER_CHUNK = 4
RATE = 46000.0
LATENCY = 1.8
ORDERS = ((0, 1, 2), (0, 2, 1), (1, 2, 0))
ROWS = 32


def half_steps(size):
    middle = size // 2
    found = []
    for direction in (1, -1):
        first, second = (0, 1) if direction == 1 else (1, 0)
        for step in range(1, middle + 1):
            if step == middle:
                found.append((direction, step, first))
            else:
                found.append((direction, step, first))
                found.append((direction, step, second))
    return found


def reduce_steps(size):
    middle = size // 2
    found = []
    for direction in (1, -1):
        first, second = (0, 1) if direction == 1 else (1, 0)
        for step in range(1, middle + 1):
            if step == 1:
                found.append((direction, step, first))
            else:
                found.append((direction, step, second))
                found.append((direction, step, first))
    return found


def simulate(copies):
    waiting = {key: set(value[2]) for key, value in copies.items()}
    readers = {}
    for key, value in copies.items():
        for other in value[2]:
            readers.setdefault(other, []).append(key)
    free = {}
    serial = 0
    heap = []
    for key in copies:
        if not waiting[key]:
            heap.append((0.0, serial, "start", key))
            serial += 1
    heapq.heapify(heap)
    order = []
    while heap:
        now, _, kind, key = heapq.heappop(heap)
        order.append((kind, key, now))
        link, size, _, delay = copies[key]
        if kind == "start":
            done = max(now, free.get(link, 0.0)) + size / RATE
            free[link] = done
            heapq.heappush(heap, (done + LATENCY, serial, "arrive", key))
            serial += 1
        else:
            for reader in readers.get(key, []):
                waiting[reader].discard(key)
                if not waiting[reader]:
                    heapq.heappush(heap, (now + delay, serial, "start", reader))
                    serial += 1
    return order


def gather_plan(sizes, widths):
    copies = {}
    for color, order in enumerate(ORDERS):
        per_block = ROWS * widths[color] * 2
        for stage in range(3):
            axis = order[stage]
            block = per_block
            for earlier in order[:stage]:
                block *= sizes[earlier]
            for direction, step, half in half_steps(sizes[axis]):
                if step > 1:
                    needs = {(color, stage, direction, step - 1, half)}
                elif stage == 0:
                    needs = set()
                else:
                    needs = set()
                    for d, s, h in half_steps(sizes[order[stage - 1]]):
                        if stage == 1 or h == half:
                            needs.add((color, stage - 1, d, s, h))
                key = (color, stage, direction, step, half)
                copies[key] = ((axis, direction), block / 2, needs, 0.0)
    return copies


def reduce_plan(sizes, widths):
    copies = {}
    for color, order in enumerate(ORDERS):
        per_block = ROWS * widths[color] * 2
        for stage in (2, 1, 0):
            axis = order[stage]
            block = per_block
            for earlier in order[:stage]:
                block *= sizes[earlier]
            last = sizes[axis] // 2
            for direction, step, half in reduce_steps(sizes[axis]):
                needs = set()
                first = 0 if direction == 1 else 1
                if step > 2 or (step == 2 and half == first):
                    needs.add((color, stage, direction, step - 1, half))
                elif stage < 2:
                    above = sizes[order[stage + 1]]
                    for d, s, h in reduce_steps(above):
                        if s == above // 2 and (stage == 0 or h == half):
                            needs.add((color, stage + 1, d, s, h))
                key = (color, stage, direction, step, half)
                copies[key] = ((axis, direction), block / 2, needs, block / 2 / 2e6)
    return copies


def make_kernel(sizes, widths, half_width, experts_here, spe):
    groups_x = 2
    nz, nx, ny = sizes
    group_tokens = groups_x * ny * ROWS
    slots = experts_here * spe
    groups = nz * (nx // groups_x)
    per_chunk = min(GROUPS_PER_CHUNK, groups)
    chunks = groups // per_chunk
    offsets = (0, widths[0], widths[0] + widths[1])
    gather_widths = (widths[0] + LANES, widths[1], widths[2])
    gather = gather_plan(sizes, gather_widths)
    gather_order = simulate(gather)
    gather_number = {key: n for n, key in enumerate(gather)}
    reduce = reduce_plan(sizes, widths)
    reduce_order = simulate(reduce)
    reduce_number = {key: n for n, key in enumerate(reduce)}
    buffers = {}
    buffer_of = {}
    for color, order in enumerate(ORDERS):
        for stage in range(3):
            steps = reduce_steps(sizes[order[stage]])
            earlier = [sizes[a] for a in sorted(order[:stage])]
            if stage == 0:
                shape = (ROWS // 2, widths[color])
            else:
                shape = []
                for a in sorted(order[:stage]):
                    shape.append(sizes[a] // 2 if a == order[0] else sizes[a])
                shape = tuple(shape) + (ROWS, widths[color])
            buffers[(color, stage)] = (len(steps),) + shape
            for n, step in enumerate(steps):
                buffer_of[(color, stage) + step] = n
    buffer_keys = sorted(buffers)

    def kernel(
        x_ref, table_ref, pick_ref, weigh_ref, code_ref, code_t_ref, gate_hbm, up_hbm, down_hbm,
        out_ref, g0, g1, g2, gate_up, down, chosen, pre, pre_out, pre_in, fin_out, fin_in,
        *rest,
    ):
        landing = dict(zip(buffer_keys, rest[: len(buffer_keys)]))
        (own_sem, pair_send, pair_recv, load_sem, load_send, load_recv,
         gather_send, gather_recv, reduce_send, reduce_recv,
         pre_send, pre_recv, fin_send, fin_recv) = rest[len(buffer_keys):]
        held = (g0, g1, g2)
        z = lax.axis_index("rep")
        e = lax.axis_index("exp")
        core = lax.rem(e, 2)
        chip = lax.div(e, 2)
        y = lax.rem(chip, ny)
        x = lax.div(chip, ny)
        here = (z, x, y)
        partner = (z, e + 1 - 2 * core)

        def neighbour(axis, direction):
            moved = list(here)
            moved[axis] = lax.rem(here[axis] + direction + sizes[axis], sizes[axis])
            return (moved[0], (moved[1] * ny + moved[2]) * 2 + core)

        barrier = pltpu.get_barrier_semaphore()
        peers = [partner] + [neighbour(a, d) for a in range(3) for d in (1, -1)]
        for peer in peers:
            pl.semaphore_signal(barrier, inc=1, device_id=peer, device_id_type=MESH)
        pl.semaphore_wait(barrier, len(peers))

        def block(color, stage, index, half, width):
            order = ORDERS[color]
            where = []
            for a in range(3):
                if a == order[stage]:
                    where.append(index)
                elif a in order[:stage]:
                    if a == order[0]:
                        where.append(pl.ds(half * (sizes[a] // 2), sizes[a] // 2))
                    else:
                        where.append(pl.ds(0, sizes[a]))
                else:
                    where.append(here[a])
            rows = pl.ds(half * (ROWS // 2), ROWS // 2) if stage == 0 else pl.ds(0, ROWS)
            return held[color].at[where[0], where[1], where[2], rows, pl.ds(0, width)]

        own_rows = pl.ds(pl.multiple_of(core * 16, 16), 16)
        own_copies, pair_copies = [], []
        for color in range(3):
            for mine in (True, False):
                side = core if mine else 1 - core
                start = pl.multiple_of(side * half_width + offsets[color], LANES)
                source = x_ref.at[:, pl.ds(start, widths[color])]
                target = held[color].at[z, x, y, own_rows, pl.ds(0, widths[color])]
                if mine:
                    own_copies.append(
                        pltpu.make_async_copy(source, target, own_sem.at[color])
                    )
                else:
                    pair_copies.append(
                        pltpu.make_async_remote_copy(
                            src_ref=source, dst_ref=target, send_sem=pair_send.at[color],
                            recv_sem=pair_recv.at[color], device_id=partner,
                            device_id_type=MESH,
                        )
                    )
        table_target = g0.at[z, x, y, own_rows, pl.ds(widths[0], LANES)]
        own_copies.append(pltpu.make_async_copy(table_ref, table_target, own_sem.at[3]))
        pair_copies.append(
            pltpu.make_async_remote_copy(
                src_ref=table_ref, dst_ref=table_target, send_sem=pair_send.at[3],
                recv_sem=pair_recv.at[3], device_id=partner, device_id_type=MESH,
            )
        )
        for copy in pair_copies:
            copy.start()
        for copy in own_copies:
            copy.start()

        local = experts_here // 2
        mine_experts = pl.ds(core * local, local)
        load_copies, send_copies = [], []
        for n, (source, target) in enumerate(
            (
                (gate_hbm, gate_up.at[mine_experts, 0]),
                (up_hbm, gate_up.at[mine_experts, 1]),
                (down_hbm, down.at[mine_experts]),
            )
        ):
            start = pl.multiple_of(core * half_width, LANES)
            other = pl.multiple_of((1 - core) * half_width, LANES)
            load_copies.append(
                pltpu.make_async_copy(
                    source.at[:, :, pl.ds(start, half_width)], target, load_sem.at[n]
                )
            )
            send_copies.append(
                pltpu.make_async_remote_copy(
                    src_ref=source.at[:, :, pl.ds(other, half_width)], dst_ref=target,
                    send_sem=load_send.at[n], recv_sem=load_recv.at[n], device_id=partner,
                    device_id_type=MESH,
                )
            )
        for copy in own_copies:
            copy.wait()
        for copy in pair_copies:
            copy.wait()
        for copy in load_copies:
            copy.start()
        for copy in send_copies:
            copy.start()

        def gather_copy(key, received):
            color, stage, direction, step, half = key
            axis = ORDERS[color][stage]
            back = step if received else step - 1
            index = lax.rem(here[axis] - direction * back + sizes[axis], sizes[axis])
            place = block(color, stage, index, half, gather_widths[color])
            n = gather_number[key]
            return pltpu.make_async_remote_copy(
                src_ref=place, dst_ref=place, send_sem=gather_send.at[n],
                recv_sem=gather_recv.at[n], device_id=neighbour(axis, direction),
                device_id_type=MESH,
            )

        for kind, key, _ in gather_order:
            if kind == "start":
                gather_copy(key, False).start()
            else:
                gather_copy(key, True).wait_recv()
        for key in gather:
            gather_copy(key, False).wait_send()
        for copy in load_copies:
            copy.wait()
        for copy in send_copies:
            copy.wait()

        def contract_last(a, b):
            return lax.dot_general(
                a, b, (((1,), (1,)), ((), ())), preferred_element_type=jnp.float32
            )

        def group_place(number):
            gz = lax.div(number, nx // groups_x)
            gx = lax.rem(number, nx // groups_x) * groups_x
            return gz, pl.ds(gx, groups_x)

        def group_table(gz, gx):
            return g0[gz, gx, :, :, pl.ds(widths[0], LANES)].reshape(group_tokens, LANES)

        def pre_copy(q):
            return pltpu.make_async_remote_copy(
                src_ref=pre_out.at[q], dst_ref=pre_in.at[q], send_sem=pre_send.at[q],
                recv_sem=pre_recv.at[q], device_id=partner, device_id_type=MESH,
            )

        def first_half(q, carry):
            def select(g, inner):
                gz, gx = group_place(q * per_chunk + g)
                codes = contract_last(pick_ref[...], group_table(gz, gx))
                onehot = (codes == code_ref[...]).astype(jnp.bfloat16)
                for color in range(3):
                    rows = held[color][gz, gx, :, :, pl.ds(0, widths[color])]
                    rows = rows.reshape(group_tokens, widths[color])
                    picked = jnp.dot(onehot, rows, preferred_element_type=jnp.float32)
                    picked = picked.astype(jnp.bfloat16)
                    for n in range(experts_here):
                        chosen[n, pl.ds(pl.multiple_of(g * spe, 16), spe),
                               pl.ds(offsets[color], widths[color])] = (
                            picked[n * spe:(n + 1) * spe]
                        )
                return inner

            lax.fori_loop(0, per_chunk, select, 0)

            def project(n, inner):
                for which in range(2):
                    value = contract_last(chosen[n], gate_up[n, which])
                    pre[q, n, which] = value
                    pre_out[q, n, which] = value.astype(jnp.bfloat16)
                return inner

            lax.fori_loop(0, experts_here, project, 0)
            pre_copy(q).start()
            return carry

        lax.fori_loop(0, chunks, first_half, 0)

        def second_half(q, carry):
            pre_copy(q).wait_recv()

            def expand(n, inner):
                gate_value = pre[q, n, 0] + pre_in[q, n, 0].astype(jnp.float32)
                up_value = pre[q, n, 1] + pre_in[q, n, 1].astype(jnp.float32)
                hidden = gate_value / (1.0 + jnp.exp(-gate_value)) * up_value
                outcome = jnp.dot(
                    hidden.astype(jnp.bfloat16), down[n], preferred_element_type=jnp.float32
                ).astype(jnp.bfloat16)
                for g in range(per_chunk):
                    chosen[g, pl.ds(pl.multiple_of(n * spe, 16), spe)] = (
                        outcome[g * spe:(g + 1) * spe]
                    )
                return inner

            lax.fori_loop(0, experts_here, expand, 0)

            def combine(g, inner):
                gz, gx = group_place(q * per_chunk + g)
                table = group_table(gz, gx)
                codes = contract_last(table, pick_ref[...])
                weights = contract_last(table, weigh_ref[...])
                scatter = jnp.where(codes == code_t_ref[...], weights, 0.0).astype(jnp.bfloat16)
                for color in range(3):
                    part = chosen[g, :, pl.ds(offsets[color], widths[color])]
                    summed = jnp.dot(scatter, part, preferred_element_type=jnp.float32)
                    held[color][gz, gx, :, :, pl.ds(0, widths[color])] = summed.astype(
                        jnp.bfloat16
                    ).reshape(groups_x, ny, ROWS, widths[color])
                return inner

            lax.fori_loop(0, per_chunk, combine, 0)
            pre_copy(q).wait_send()
            return carry

        lax.fori_loop(0, chunks, second_half, 0)

        def reduce_copy(key):
            color, stage, direction, step, half = key
            axis = ORDERS[color][stage]
            size = sizes[axis]
            index = lax.rem(here[axis] + direction * (size // 2 - step + 1) + size, size)
            n = reduce_number[key]
            return pltpu.make_async_remote_copy(
                src_ref=block(color, stage, index, half, widths[color]),
                dst_ref=landing[(color, stage)].at[buffer_of[key]],
                send_sem=reduce_send.at[n], recv_sem=reduce_recv.at[n],
                device_id=neighbour(axis, direction), device_id_type=MESH,
            )

        def add_into(target, sources):
            lead = target.shape[:-2]
            if not lead:
                total = target[...].astype(jnp.float32)
                for source in sources:
                    total = total + source[...].astype(jnp.float32)
                target[...] = total.astype(jnp.bfloat16)
                return
            inner_size = lead[1] if len(lead) > 1 else 1

            def one(n, carry):
                if len(lead) == 1:
                    where = (n,)
                else:
                    where = (lax.div(n, inner_size), lax.rem(n, inner_size))
                total = target[where].astype(jnp.float32)
                for source in sources:
                    total = total + source[where].astype(jnp.float32)
                target[where] = total.astype(jnp.bfloat16)
                return carry

            lax.fori_loop(0, lead[0] * inner_size, one, 0)

        arrived = set()
        for kind, key, _ in reduce_order:
            if kind == "start":
                reduce_copy(key).start()
                continue
            reduce_copy(key).wait_recv()
            arrived.add(key)
            color, stage, direction, step, half = key
            axis = ORDERS[color][stage]
            size = sizes[axis]
            last = size // 2
            if step < last:
                index = lax.rem(here[axis] + direction * (last - step) + size, size)
                target = block(color, stage, index, half, widths[color])
                add_into(target, [landing[(color, stage)].at[buffer_of[key]]])
                continue
            parts = [
                k for k in reduce
                if k[0] == color and k[1] == stage and k[3] == last and k[4] == half
            ]
            if all(k in arrived for k in parts):
                target = block(color, stage, here[axis], half, widths[color])
                add_into(target, [landing[(color, stage)].at[buffer_of[k]] for k in parts])

        other_rows = pl.ds(pl.multiple_of((1 - core) * 16, 16), 16)
        for color in range(3):
            columns = pl.ds(offsets[color], widths[color])
            fin_out[:, columns] = held[color][z, x, y, other_rows, pl.ds(0, widths[color])]
        last_copy = pltpu.make_async_remote_copy(
            src_ref=fin_out, dst_ref=fin_in, send_sem=fin_send, recv_sem=fin_recv,
            device_id=partner, device_id_type=MESH,
        )
        last_copy.start()
        for color in range(3):
            start = pl.multiple_of(core * half_width + offsets[color], LANES)
            out_ref[:, pl.ds(start, widths[color])] = held[color][
                z, x, y, own_rows, pl.ds(0, widths[color])
            ]
        for key in reduce:
            reduce_copy(key).wait_send()
        last_copy.wait()
        out_ref[:, pl.ds(pl.multiple_of((1 - core) * half_width, LANES), half_width)] = fin_in[...]

    shared = dict(
        gather=len(gather), reduce=len(reduce), chunks=chunks, per_chunk=per_chunk,
        gather_widths=gather_widths, buffers=[buffers[k] for k in buffer_keys],
        group_tokens=group_tokens, slots=slots,
    )
    return kernel, shared


def routing_table(routed_experts, route_weights, expert_count):
    onehot = routed_experts[:, :, None] == jnp.arange(expert_count, dtype=jnp.int32)
    named = jnp.any(onehot, axis=1).astype(jnp.float32)
    rank = jnp.cumsum(named, axis=0)
    weights = jnp.sum(jnp.where(onehot, route_weights[:, :, None], 0.0), axis=1)
    table = jnp.concatenate([named * rank, weights], axis=1)
    pad = LANES - table.shape[1]
    return jnp.pad(table, ((0, 0), (0, pad))).astype(jnp.bfloat16)


def solution(mesh):
    nz = mesh.shape["rep"]
    nx = int(round((mesh.shape["exp"] // 2) ** 0.5))
    ny = mesh.shape["exp"] // 2 // nx
    sizes = (nz, nx, ny)

    def on_device(tokens, routed_experts, route_weights, gate_weight, up_weight, down_weight):
        token_rows, width = tokens.shape
        local, units = gate_weight.shape[:2]
        expert_count = local * mesh.shape["exp"]
        experts_here = 2 * local
        half_width = width // 2
        tiles = half_width // LANES
        thin = max(1, 5 * tiles // 16) * LANES
        widths = (thin, thin, half_width - 2 * thin)
        spe = CAPACITY * (2 * ny * ROWS // token_rows)
        kernel, info = make_kernel(sizes, widths, half_width, experts_here, spe)
        slots, group_tokens = info["slots"], info["group_tokens"]
        chunks, per_chunk = info["chunks"], info["per_chunk"]

        table = routing_table(routed_experts, route_weights, expert_count)
        chip = lax.axis_index("exp") // 2
        slot = jnp.arange(slots, dtype=jnp.int32)
        lane = jnp.arange(LANES, dtype=jnp.int32)
        expert_of = chip * experts_here + slot // spe
        pick = (lane[None, :] == expert_of[:, None]).astype(jnp.bfloat16)
        weigh = (lane[None, :] == expert_of[:, None] + expert_count).astype(jnp.bfloat16)
        block_of_token = jnp.arange(group_tokens, dtype=jnp.int32) // token_rows
        block_of_slot = (slot % spe) // CAPACITY
        code = jnp.where(
            block_of_slot[:, None] == block_of_token[None, :], (slot % CAPACITY + 1)[:, None], -1
        ).astype(jnp.float32)

        bf16 = jnp.bfloat16
        dma = pltpu.SemaphoreType.DMA
        vmem = pl.BlockSpec(memory_space=pltpu.VMEM)
        hbm = pl.BlockSpec(memory_space=pl.ANY)
        return pl.pallas_call(
            kernel,
            out_shape=jax.ShapeDtypeStruct((token_rows, width), bf16),
            in_specs=[vmem] * 6 + [hbm] * 3,
            out_specs=vmem,
            scratch_shapes=[
                *[pltpu.VMEM((nz, nx, ny, ROWS, w), bf16) for w in info["gather_widths"]],
                pltpu.VMEM((experts_here, 2, units, half_width), bf16),
                pltpu.VMEM((experts_here, units, half_width), bf16),
                pltpu.VMEM((max(experts_here, per_chunk), max(slots, per_chunk * spe), half_width), bf16),
                pltpu.VMEM((chunks, experts_here, 2, per_chunk * spe, units), jnp.float32),
                pltpu.VMEM((chunks, experts_here, 2, per_chunk * spe, units), bf16),
                pltpu.VMEM((chunks, experts_here, 2, per_chunk * spe, units), bf16),
                pltpu.VMEM((token_rows, half_width), bf16),
                pltpu.VMEM((token_rows, half_width), bf16),
                *[pltpu.VMEM(shape, bf16) for shape in info["buffers"]],
                dma((4,)), dma((4,)), dma((4,)), dma((3,)), dma((3,)), dma((3,)),
                dma((info["gather"],)), dma((info["gather"],)),
                dma((info["reduce"],)), dma((info["reduce"],)),
                dma((chunks,)), dma((chunks,)), dma(()), dma(()),
            ],
            compiler_params=pltpu.CompilerParams(
                collective_id=0, has_side_effects=True, vmem_limit_bytes=67_000_000
            ),
        )(tokens, table, pick, weigh, code, code.T, gate_weight, up_weight, down_weight)

    placed = (
        P(("rep", "exp"), None),
        P(("rep", "exp"), None),
        P(("rep", "exp"), None),
        P("exp", "rep", None),
        P("exp", "rep", None),
        P("exp", "rep", None),
    )
    return jax.shard_map(
        on_device, mesh=mesh, in_specs=placed, out_specs=P(("rep", "exp"), None), check_vma=False
    )
```

```python
import heapq

import jax
import jax.numpy as jnp
import numpy as np
from jax import lax
from jax.experimental import pallas as pl
from jax.experimental.pallas import tpu as pltpu
from jax.sharding import PartitionSpec as P

MESH = pl.DeviceIdType.MESH
LANES = 128
CAPACITY = 3
PHASES = 2
HALVES = 2
ORDERS = ((0, 1, 2), (0, 2, 1), (1, 2, 0))
LONG = (1, -1, 1)
RATE = 46000.0
PAIR_RATE = 150000.0
LATENCY = 1.8
LOOK = 4.0
ADD_RATE = 1.5e6
COSTS = {"select": 0.85, "project": 2.5, "expand": 1.9, "combine": 1.9}


def steps_of(size, split, long, gathering):
    middle = size // 2
    odd_step = middle if gathering else 1
    found = []
    for step in range(1, middle + 1):
        for direction in (1, -1):
            if split:
                first = 0 if direction == 1 else 1
                both = (first, 1 - first) if gathering else (1 - first, first)
                for half in both:
                    if step != odd_step or half == first:
                        found.append((direction, step, half))
            elif step != odd_step or direction == long:
                found.append((direction, step, 0))
    return found


def block_bytes(sizes, width, rows, order, stage):
    total = rows * width * 2
    for axis in order[:stage]:
        total *= sizes[axis]
    return total // 2 if stage else total


def build_tasks(sizes, gather_widths, reduce_widths, rows, exchange_bytes):
    tasks = {}
    chunk_before = None
    for p in range(PHASES):
        arrivals = {}
        for c, order in enumerate(ORDERS):
            for stage in range(3):
                axis = order[stage]
                for d, s, h in steps_of(sizes[axis], stage > 0, LONG[c], True):
                    if s > 1:
                        needs = {("g", p, c, stage, d, s - 1, h)}
                    elif stage == 0:
                        needs = set()
                    else:
                        needs = {
                            k for k in tasks
                            if k[:4] == ("g", p, c, stage - 1) and (stage == 1 or k[6] == h)
                        }
                    key = ("g", p, c, stage, d, s, h)
                    size = block_bytes(sizes, gather_widths[p][c], rows, order, stage)
                    tasks[key] = ((axis, d), size, needs)
            arrivals[c] = {k for k in tasks if k[:4] == ("g", p, c, 2)}
        for q in range(HALVES):
            for c in range(3):
                needs = set(arrivals[2])
                if c < 2:
                    needs |= {k for k in arrivals[c] if k[6] == q}
                if chunk_before is not None:
                    needs.add(("project",) + chunk_before)
                tasks[("select", p, q, c)] = (None, COSTS["select"], needs)
            tasks[("project", p, q)] = (
                None, COSTS["project"], {("select", p, q, c) for c in range(3)}
            )
            tasks[("x", p, q)] = (("pair", 0), exchange_bytes, {("project", p, q)})
            needs = {("x", p, q)}
            if chunk_before is not None:
                needs.add(("combine",) + chunk_before)
            tasks[("expand", p, q)] = (None, COSTS["expand"], needs)
            tasks[("combine", p, q)] = (None, COSTS["combine"], {("expand", p, q)})
            chunk_before = (p, q)
        for c, order in enumerate(ORDERS):
            for stage in (2, 1, 0):
                axis = order[stage]
                steps = steps_of(sizes[axis], stage > 0, LONG[c], False)
                for d, s, h in steps:
                    if (d, s - 1, h) in steps:
                        needs = {("r", p, c, stage, d, s - 1, h)}
                    elif stage == 2:
                        needs = {("combine", p, q) for q in range(HALVES) if c == 2 or q == h}
                    else:
                        needs = {
                            k for k in tasks
                            if k[:4] == ("r", p, c, stage + 1)
                            and k[5] == sizes[order[stage + 1]] // 2
                            and (stage == 0 or k[6] == h)
                        }
                    key = ("r", p, c, stage, d, s, h)
                    size = block_bytes(sizes, reduce_widths[p][c], rows, order, stage)
                    tasks[key] = ((axis, d), size, needs)
    return tasks


def priority(key):
    if key[0] == "g":
        return key[1] * 10 + key[3]
    if key[0] == "r":
        return 20 + key[1] * 10 + key[3]
    return key[1] + {"select": 40, "project": 40, "x": 0, "expand": 10, "combine": 10}[key[0]]


def schedule(tasks):
    waiting = {k: set(v[2]) for k, v in tasks.items()}
    readers = {}
    for k, v in tasks.items():
        for other in v[2]:
            readers.setdefault(other, []).append(k)
    place = {k: n for n, k in enumerate(tasks)}
    free, pending, arriving, computing, order = {}, {}, [], [], []
    now = 0.0

    def ready(k):
        link = tasks[k][0]
        queue = computing if link is None else pending.setdefault(link, [])
        heapq.heappush(queue, (priority(k), place[k], k))

    def pump():
        for link, queue in pending.items():
            while queue and free.get(link, 0.0) - now < LOOK:
                k = heapq.heappop(queue)[2]
                order.append(("start", k))
                rate = PAIR_RATE if link[0] == "pair" else RATE
                free[link] = max(now, free.get(link, 0.0)) + tasks[k][1] / rate
                heapq.heappush(arriving, (free[link] + LATENCY, place[k], k))

    def finish(k):
        for reader in readers.get(k, ()):
            waiting[reader].discard(k)
            if not waiting[reader]:
                ready(reader)

    for k in tasks:
        if not waiting[k]:
            ready(k)
    pump()
    while arriving or computing:
        if arriving and (arriving[0][0] <= now or not computing):
            when, _, k = heapq.heappop(arriving)
            now = max(now, when) + 0.03
            if k[0] == "r":
                now += tasks[k][1] / ADD_RATE
            order.append(("arrive", k))
        else:
            k = heapq.heappop(computing)[2]
            now += tasks[k][1]
            order.append(("compute", k))
        finish(k)
        pump()
    return order, now


def make_kernel(sizes, unit, rows, experts_here, units):
    nz, nx, ny = sizes
    half_width = 3 * unit + LANES
    wide = unit + LANES
    reduce_widths = ((wide, unit, unit), (unit, wide, unit))
    gather_widths = ((wide, unit, wide), (unit, wide, wide))
    segments = (
        (((0, 0, wide),), ((0, wide, unit),), ((0, wide + unit, unit),)),
        (((0, 0, unit),), ((0, wide, unit), (unit, unit, LANES)), ((0, wide + unit, unit),)),
    )
    per_chunk = nz // HALVES
    spe = CAPACITY * nx * ny
    slots = experts_here * spe
    chunk_rows = per_chunk * spe
    group_tokens = nx * ny * rows
    exchange_bytes = experts_here * 2 * chunk_rows * units * 2
    tasks = build_tasks(sizes, gather_widths, reduce_widths, rows, exchange_bytes)
    order, _ = schedule(tasks)
    gathers = [k for k in tasks if k[0] == "g"]
    reduces = [k for k in tasks if k[0] == "r"]
    number = {k: n for n, k in enumerate(gathers)}
    number.update({k: n for n, k in enumerate(reduces)})
    buffers, buffer_of = {}, {}
    for k in reduces:
        p, c, stage = k[1:4]
        first = ORDERS[c][0]
        shape = []
        for a in sorted(ORDERS[c][:stage]):
            shape.append(sizes[a] // 2 if a == first else sizes[a])
        count = buffers.get((p, c, stage), (0,))[0]
        buffer_of[k] = count
        buffers[(p, c, stage)] = (count + 1,) + tuple(shape) + (rows, reduce_widths[p][c])
    buffer_keys = sorted(buffers)

    def kernel(
        x_ref, ids_ref, weight_ref, lane_ref, code_ref, code_t_ref, gate_hbm, up_hbm, down_hbm,
        out_ref, held01, held2, table_ref, gate_up, down, chosen, outs, pre_out, pre_in, fin_in,
        *rest,
    ):
        landing = dict(zip(buffer_keys, rest[: len(buffer_keys)]))
        (own_sem, pair_send, pair_recv, load_sem, load_send, load_recv,
         gather_send, gather_recv, reduce_send, reduce_recv,
         pre_send, pre_recv, fin_send, fin_recv) = rest[len(buffer_keys):]
        z = lax.axis_index("rep")
        e = lax.axis_index("exp")
        core = lax.rem(e, 2)
        chip = lax.div(e, 2)
        y = lax.rem(chip, ny)
        x = lax.div(chip, ny)
        here = (z, x, y)
        partner = (z, e + 1 - 2 * core)

        def held(p, c):
            return held2.at[p] if c == 2 else held01.at[c, p]

        def neighbour(axis, direction):
            moved = list(here)
            moved[axis] = lax.rem(here[axis] + direction + sizes[axis], sizes[axis])
            return (moved[0], (moved[1] * ny + moved[2]) * 2 + core)

        barrier = pltpu.get_barrier_semaphore()
        peers = [partner] + [neighbour(a, d) for a in range(3) for d in (1, -1)]
        for peer in peers:
            pl.semaphore_signal(barrier, inc=1, device_id=peer, device_id_type=MESH)

        experts = LANES // 2
        lane = lax.broadcasted_iota(jnp.int32, (rows, LANES), 1)
        named = jnp.zeros((rows, LANES), jnp.float32)
        weights = jnp.zeros((rows, LANES), jnp.float32)
        for k in range(ids_ref.shape[1]):
            name = ids_ref[:, k:k + 1]
            named = named + (lane == name).astype(jnp.float32)
            weights = weights + jnp.where(lane == name + experts, weight_ref[:, k:k + 1], 0.0)
        below = lax.broadcasted_iota(jnp.int32, (rows, rows), 0)
        across = lax.broadcasted_iota(jnp.int32, (rows, rows), 1)
        triangle = (across <= below).astype(jnp.bfloat16)
        rank = jnp.dot(triangle, named.astype(jnp.bfloat16), preferred_element_type=jnp.float32)
        table_ref[...] = (named * rank + weights).astype(jnp.bfloat16)

        pl.semaphore_wait(barrier, len(peers))

        def pieces(phase):
            mine = (z, x, y, pl.ds(0, rows))
            return (
                (0, unit, held01.at[(0, phase) + mine + (pl.ds(0, unit),)]),
                (unit, LANES, held01.at[(phase, phase) + mine + (pl.ds(unit, LANES),)]),
                (wide, unit, held01.at[(1, phase) + mine + (pl.ds(0, unit),)]),
                (wide + unit, unit, held2.at[(phase,) + mine + (pl.ds(0, unit),)]),
            )

        table_place = held2.at[core, z, x, y, pl.ds(0, rows), pl.ds(unit, LANES)]
        own_copies, pair_copies = [], []
        for n, (column, width, place) in enumerate(pieces(core)):
            start = pl.multiple_of(core * half_width + column, LANES)
            other = pl.multiple_of((1 - core) * half_width + column, LANES)
            own_copies.append((x_ref.at[:, pl.ds(start, width)], place))
            pair_copies.append((x_ref.at[:, pl.ds(other, width)], place))
        own_copies.append((table_ref, table_place))
        pair_copies.append((table_ref, table_place))
        own_copies = [
            pltpu.make_async_copy(a, b, own_sem.at[n]) for n, (a, b) in enumerate(own_copies)
        ]
        pair_copies = [
            pltpu.make_async_remote_copy(
                src_ref=a, dst_ref=b, send_sem=pair_send.at[n], recv_sem=pair_recv.at[n],
                device_id=partner, device_id_type=MESH,
            )
            for n, (a, b) in enumerate(pair_copies)
        ]
        for copy in pair_copies + own_copies:
            copy.start()

        local = experts_here // 2
        mine_experts = pl.ds(core * local, local)
        loads, sends = [], []
        for n, (source, target) in enumerate(
            (
                (gate_hbm, gate_up.at[mine_experts, 0]),
                (up_hbm, gate_up.at[mine_experts, 1]),
                (down_hbm, down.at[mine_experts]),
            )
        ):
            start = pl.multiple_of(core * half_width, LANES)
            other = pl.multiple_of((1 - core) * half_width, LANES)
            loads.append(
                pltpu.make_async_copy(
                    source.at[:, :, pl.ds(start, half_width)], target, load_sem.at[n]
                )
            )
            sends.append(
                pltpu.make_async_remote_copy(
                    src_ref=source.at[:, :, pl.ds(other, half_width)], dst_ref=target,
                    send_sem=load_send.at[n], recv_sem=load_recv.at[n], device_id=partner,
                    device_id_type=MESH,
                )
            )
        for copy in own_copies + pair_copies:
            copy.wait()
        for copy in loads + sends:
            copy.start()

        def block(p, c, stage, index, half, width):
            axes = ORDERS[c]
            where = []
            for a in range(3):
                if a == axes[stage]:
                    where.append(index)
                elif a in axes[:stage]:
                    if a == axes[0]:
                        where.append(pl.ds(half * (sizes[a] // 2), sizes[a] // 2))
                    else:
                        where.append(pl.ds(0, sizes[a]))
                else:
                    where.append(here[a])
            lead = (p,) if c == 2 else (c, p)
            ref = held2 if c == 2 else held01
            return ref.at[lead + tuple(where) + (pl.ds(0, rows), pl.ds(0, width))]

        def gather_copy(key, received):
            _, p, c, stage, d, s, h = key
            axis = ORDERS[c][stage]
            back = s if received else s - 1
            index = lax.rem(here[axis] - d * back + sizes[axis], sizes[axis])
            place = block(p, c, stage, index, h, gather_widths[p][c])
            n = number[key]
            return pltpu.make_async_remote_copy(
                src_ref=place, dst_ref=place, send_sem=gather_send.at[n],
                recv_sem=gather_recv.at[n], device_id=neighbour(axis, d), device_id_type=MESH,
            )

        def reduce_copy(key):
            _, p, c, stage, d, s, h = key
            axis = ORDERS[c][stage]
            size = sizes[axis]
            index = lax.rem(here[axis] + d * (size // 2 - s + 1) + size, size)
            n = number[key]
            return pltpu.make_async_remote_copy(
                src_ref=block(p, c, stage, index, h, reduce_widths[p][c]),
                dst_ref=landing[(p, c, stage)].at[buffer_of[key]],
                send_sem=reduce_send.at[n], recv_sem=reduce_recv.at[n],
                device_id=neighbour(axis, d), device_id_type=MESH,
            )

        def pre_copy(p, q):
            n = p * HALVES + q
            return pltpu.make_async_remote_copy(
                src_ref=pre_out.at[n], dst_ref=pre_in.at[n], send_sem=pre_send.at[n],
                recv_sem=pre_recv.at[n], device_id=partner, device_id_type=MESH,
            )

        def contract_last(a, b):
            return lax.dot_general(
                a, b, (((1,), (1,)), ((), ())), preferred_element_type=jnp.float32
            )

        base = chip * experts_here

        def group(p, c, gz, start, width):
            lead = (p,) if c == 2 else (c, p)
            ref = held2 if c == 2 else held01
            value = ref[lead + (gz, slice(None), slice(None), slice(None), pl.ds(start, width))]
            return value.reshape(group_tokens, width)

        def select(p, q, c):
            def one(g, carry):
                gz = q * per_chunk + g
                pick = (lane_ref[...] == base).astype(jnp.bfloat16)
                codes = contract_last(pick, group(p, 2, gz, unit, LANES))
                onehot = (codes == code_ref[...]).astype(jnp.bfloat16)
                for start, column, width in segments[p][c]:
                    picked = jnp.dot(
                        onehot, group(p, c, gz, start, width), preferred_element_type=jnp.float32
                    ).astype(jnp.bfloat16)
                    for n in range(experts_here):
                        chosen[n, pl.ds(pl.multiple_of(g * spe, 16), spe), pl.ds(column, width)] = (
                            picked[n * spe:(n + 1) * spe]
                        )
                return carry

            lax.fori_loop(0, per_chunk, one, 0)

        def project(p, q):
            def one(n, carry):
                for which in range(2):
                    pre_out[p * HALVES + q, n, which] = contract_last(
                        chosen[n], gate_up[n, which]
                    ).astype(jnp.bfloat16)
                return carry

            lax.fori_loop(0, experts_here, one, 0)

        def expand(p, q):
            index = p * HALVES + q

            def one(n, carry):
                values = []
                for which in range(2):
                    mine = pre_out[index, n, which].astype(jnp.float32)
                    values.append(mine + pre_in[index, n, which].astype(jnp.float32))
                hidden = values[0] / (1.0 + jnp.exp(-values[0])) * values[1]
                outcome = jnp.dot(
                    hidden.astype(jnp.bfloat16), down[n], preferred_element_type=jnp.float32
                ).astype(jnp.bfloat16)
                for g in range(per_chunk):
                    outs[g, pl.ds(pl.multiple_of(n * spe, 16), spe)] = (
                        outcome[g * spe:(g + 1) * spe]
                    )
                return carry

            lax.fori_loop(0, experts_here, one, 0)

        def combine(p, q):
            def one(g, carry):
                gz = q * per_chunk + g
                table = group(p, 2, gz, unit, LANES)
                pick = (lane_ref[...] == base).astype(jnp.bfloat16)
                weigh = (lane_ref[...] == base + experts).astype(jnp.bfloat16)
                codes = contract_last(table, pick)
                values = contract_last(table, weigh)
                scatter = jnp.where(codes == code_t_ref[...], values, 0.0).astype(jnp.bfloat16)
                for c in range(3):
                    lead = (p,) if c == 2 else (c, p)
                    ref = held2 if c == 2 else held01
                    for start, column, width in segments[p][c]:
                        summed = jnp.dot(
                            scatter, outs[g, :, pl.ds(column, width)],
                            preferred_element_type=jnp.float32,
                        )
                        where = lead + (gz, slice(None), slice(None), slice(None))
                        ref[where + (pl.ds(start, width),)] = summed.astype(jnp.bfloat16).reshape(
                            nx, ny, rows, width
                        )
                return carry

            lax.fori_loop(0, per_chunk, one, 0)

        def add_into(target, sources):
            lead = target.shape[:-2]

            def one_block(where):
                total = target[where].astype(jnp.float32)
                for source in sources:
                    total = total + source[where].astype(jnp.float32)
                target[where] = total.astype(jnp.bfloat16)

            if not lead:
                one_block(...)
                return

            def one(n, carry):
                if len(lead) == 1:
                    one_block((n,))
                else:
                    for m in range(lead[1]):
                        one_block((n, m))
                return carry

            lax.fori_loop(0, lead[0], one, 0)

        arrived = set()

        def reduce_arrival(key):
            reduce_copy(key).wait_recv()
            arrived.add(key)
            _, p, c, stage, d, s, h = key
            axis = ORDERS[c][stage]
            size = sizes[axis]
            last = size // 2
            width = reduce_widths[p][c]
            if s < last:
                index = lax.rem(here[axis] + d * (last - s) + size, size)
                add_into(
                    block(p, c, stage, index, h, width),
                    [landing[(p, c, stage)].at[buffer_of[key]]],
                )
                return
            parts = [k for k in reduces if k[:4] == key[:4] and k[5] == last and k[6] == h]
            if all(k in arrived for k in parts):
                add_into(
                    block(p, c, stage, here[axis], h, width),
                    [landing[(p, c, stage)].at[buffer_of[k]] for k in parts],
                )

        loaded = set()
        for kind, key in order:
            if kind == "start":
                if key[0] == "g":
                    gather_copy(key, False).start()
                elif key[0] == "r":
                    reduce_copy(key).start()
                else:
                    pre_copy(key[1], key[2]).start()
            elif kind == "arrive":
                if key[0] == "g":
                    gather_copy(key, True).wait_recv()
                elif key[0] == "r":
                    reduce_arrival(key)
                else:
                    pre_copy(key[1], key[2]).wait_recv()
            elif key[0] == "select":
                select(*key[1:])
            elif key[0] == "project":
                if not loaded:
                    loaded.add("all")
                    for copy in loads + sends:
                        copy.wait()
                project(*key[1:])
            elif key[0] == "expand":
                expand(*key[1:])
            else:
                if key[2] == 0:
                    for k in gathers:
                        if k[1] == key[1]:
                            gather_copy(k, False).wait_send()
                combine(*key[1:])

        last_copies = [
            pltpu.make_async_remote_copy(
                src_ref=place, dst_ref=fin_in.at[:, pl.ds(column, width)], send_sem=fin_send.at[n],
                recv_sem=fin_recv.at[n], device_id=partner, device_id_type=MESH,
            )
            for n, (column, width, place) in enumerate(pieces(1 - core))
        ]
        for copy in last_copies:
            copy.start()
        for column, width, place in pieces(core):
            start = pl.multiple_of(core * half_width + column, LANES)
            out_ref[:, pl.ds(start, width)] = place[...]
        for k in reduces:
            reduce_copy(k).wait_send()
        for p in range(PHASES):
            for q in range(HALVES):
                pre_copy(p, q).wait_send()
        for copy in last_copies:
            copy.wait()
        out_ref[:, pl.ds(pl.multiple_of((1 - core) * half_width, LANES), half_width)] = fin_in[...]

    bf16 = jnp.bfloat16
    dma = pltpu.SemaphoreType.DMA
    chunks = PHASES * HALVES
    pre_shape = (chunks, experts_here, 2, chunk_rows, units)
    scratch = [
        pltpu.VMEM((2, PHASES, nz, nx, ny, rows, wide), bf16),
        pltpu.VMEM((PHASES, nz, nx, ny, rows, wide), bf16),
        pltpu.VMEM((rows, LANES), bf16),
        pltpu.VMEM((experts_here, 2, units, half_width), bf16),
        pltpu.VMEM((experts_here, units, half_width), bf16),
        pltpu.VMEM((experts_here, chunk_rows, half_width), bf16),
        pltpu.VMEM((per_chunk, slots, half_width), bf16),
        pltpu.VMEM(pre_shape, bf16),
        pltpu.VMEM(pre_shape, bf16),
        pltpu.VMEM((rows, half_width), bf16),
        *[pltpu.VMEM(buffers[k], bf16) for k in buffer_keys],
        dma((5,)), dma((5,)), dma((5,)), dma((3,)), dma((3,)), dma((3,)),
        dma((len(gathers),)), dma((len(gathers),)), dma((len(reduces),)), dma((len(reduces),)),
        dma((chunks,)), dma((chunks,)), dma((4,)), dma((4,)),
    ]
    slot = np.arange(slots)
    token = np.arange(group_tokens)
    lane_constant = (np.arange(LANES)[None, :] - (slot // spe)[:, None]).astype(np.int32)
    same = (slot % spe // CAPACITY)[:, None] == (token // rows)[None, :]
    code = np.where(same, (slot % CAPACITY + 1)[:, None], -1).astype(np.float32)
    return kernel, scratch, (lane_constant, code, np.ascontiguousarray(code.T))


def solution(mesh):
    nz = mesh.shape["rep"]
    nx = int(round((mesh.shape["exp"] // 2) ** 0.5))
    ny = mesh.shape["exp"] // 2 // nx

    def on_device(tokens, routed_experts, route_weights, gate_weight, up_weight, down_weight):
        rows, width = tokens.shape
        local, units = gate_weight.shape[:2]
        unit = (width // 2 // LANES - 1) // 3 * LANES
        kernel, scratch, constants = make_kernel((nz, nx, ny), unit, rows, 2 * local, units)
        vmem = pl.BlockSpec(memory_space=pltpu.VMEM)
        hbm = pl.BlockSpec(memory_space=pl.ANY)
        return pl.pallas_call(
            kernel,
            out_shape=jax.ShapeDtypeStruct((rows, width), jnp.bfloat16),
            in_specs=[vmem] * 6 + [hbm] * 3,
            out_specs=vmem,
            scratch_shapes=scratch,
            compiler_params=pltpu.CompilerParams(
                collective_id=0, has_side_effects=True, vmem_limit_bytes=67_000_000
            ),
        )(tokens, routed_experts, route_weights, *constants, gate_weight, up_weight, down_weight)

    placed = (
        P(("rep", "exp"), None),
        P(("rep", "exp"), None),
        P(("rep", "exp"), None),
        P("exp", "rep", None),
        P("exp", "rep", None),
        P("exp", "rep", None),
    )
    return jax.shard_map(
        on_device, mesh=mesh, in_specs=placed, out_specs=P(("rep", "exp"), None), check_vma=False
    )
```

```python
import heapq

import jax
import jax.numpy as jnp
import numpy as np
from jax import lax
from jax.experimental import pallas as pl
from jax.experimental.pallas import tpu as pltpu
from jax.sharding import PartitionSpec as P

MESH = pl.DeviceIdType.MESH
LANES = 128
CAPACITY = 3
PHASES = 2
HALVES = 2
ORDERS = ((0, 1, 2), (0, 2, 1), (1, 2, 0))
LONG = (1, -1, 1)
RATE = 46000.0
PAIR_RATE = 150000.0
LATENCY = 1.8
LOOK = 2.0
ADD_RATE = 1.5e6
COSTS = {"select": 0.85, "project": 2.5, "expand": 1.9, "combine": 1.9}


def steps_of(size, split, long, gathering):
    middle = size // 2
    odd_step = middle if gathering else 1
    found = []
    for step in range(1, middle + 1):
        for direction in (1, -1):
            if split:
                first = 0 if direction == 1 else 1
                both = (first, 1 - first) if gathering else (1 - first, first)
                for half in both:
                    if step != odd_step or half == first:
                        found.append((direction, step, half))
            elif step != odd_step or direction == long:
                found.append((direction, step, 0))
    return found


def block_bytes(sizes, width, rows, order, stage):
    total = rows * width * 2
    for axis in order[:stage]:
        total *= sizes[axis]
    return total // 2 if stage else total


def build_tasks(sizes, gather_widths, reduce_widths, rows, exchange_bytes):
    tasks = {}
    chunk_before = None
    for p in range(PHASES):
        arrivals = {}
        for c, order in enumerate(ORDERS):
            for stage in range(3):
                axis = order[stage]
                for d, s, h in steps_of(sizes[axis], stage > 0, LONG[c], True):
                    if s > 1:
                        needs = {("g", p, c, stage, d, s - 1, h)}
                    elif stage == 0:
                        needs = set()
                    else:
                        needs = {
                            k for k in tasks
                            if k[:4] == ("g", p, c, stage - 1) and (stage == 1 or k[6] == h)
                        }
                    key = ("g", p, c, stage, d, s, h)
                    size = block_bytes(sizes, gather_widths[p][c], rows, order, stage)
                    tasks[key] = ((axis, d), size, needs)
            arrivals[c] = {k for k in tasks if k[:4] == ("g", p, c, 2)}
        for q in range(HALVES):
            for c in range(3):
                needs = set(arrivals[2])
                if c < 2:
                    needs |= {k for k in arrivals[c] if k[6] == q}
                if chunk_before is not None:
                    needs.add(("project",) + chunk_before)
                tasks[("select", p, q, c)] = (None, COSTS["select"], needs)
            tasks[("project", p, q)] = (
                None, COSTS["project"], {("select", p, q, c) for c in range(3)}
            )
            tasks[("x", p, q)] = (("pair", 0), exchange_bytes, {("project", p, q)})
            needs = {("x", p, q)}
            if chunk_before is not None:
                needs.add(("combine",) + chunk_before)
            tasks[("expand", p, q)] = (None, COSTS["expand"], needs)
            tasks[("combine", p, q)] = (None, COSTS["combine"], {("expand", p, q)})
            chunk_before = (p, q)
        for c, order in enumerate(ORDERS):
            for stage in (2, 1, 0):
                axis = order[stage]
                steps = steps_of(sizes[axis], stage > 0, LONG[c], False)
                for d, s, h in steps:
                    if (d, s - 1, h) in steps:
                        needs = {("r", p, c, stage, d, s - 1, h)}
                    elif stage == 2:
                        needs = {("combine", p, q) for q in range(HALVES) if c == 2 or q == h}
                    else:
                        needs = {
                            k for k in tasks
                            if k[:4] == ("r", p, c, stage + 1)
                            and k[5] == sizes[order[stage + 1]] // 2
                            and (stage == 0 or k[6] == h)
                        }
                    key = ("r", p, c, stage, d, s, h)
                    size = block_bytes(sizes, reduce_widths[p][c], rows, order, stage)
                    tasks[key] = ((axis, d), size, needs)
    return tasks


def priority(key):
    if key[0] == "g":
        return key[1] * 10 + key[3]
    if key[0] == "r":
        return 20 + key[1] * 10 + key[3]
    return key[1] + {"select": 40, "project": 40, "x": 0, "expand": 10, "combine": 10}[key[0]]


def schedule(tasks):
    waiting = {k: set(v[2]) for k, v in tasks.items()}
    readers = {}
    for k, v in tasks.items():
        for other in v[2]:
            readers.setdefault(other, []).append(k)
    place = {k: n for n, k in enumerate(tasks)}
    free, pending, arriving, computing, order = {}, {}, [], [], []
    now = 0.0

    def ready(k):
        link = tasks[k][0]
        queue = computing if link is None else pending.setdefault(link, [])
        heapq.heappush(queue, (priority(k), place[k], k))

    def pump():
        for link, queue in pending.items():
            while queue and free.get(link, 0.0) - now < LOOK:
                k = heapq.heappop(queue)[2]
                order.append(("start", k))
                rate = PAIR_RATE if link[0] == "pair" else RATE
                free[link] = max(now, free.get(link, 0.0)) + tasks[k][1] / rate
                heapq.heappush(arriving, (free[link] + LATENCY, place[k], k))

    def finish(k):
        for reader in readers.get(k, ()):
            waiting[reader].discard(k)
            if not waiting[reader]:
                ready(reader)

    for k in tasks:
        if not waiting[k]:
            ready(k)
    pump()
    while arriving or computing:
        if arriving and (arriving[0][0] <= now or not computing):
            when, _, k = heapq.heappop(arriving)
            now = max(now, when) + 0.03
            if k[0] == "r":
                now += tasks[k][1] / ADD_RATE
            order.append(("arrive", k))
        else:
            k = heapq.heappop(computing)[2]
            now += tasks[k][1]
            order.append(("compute", k))
        finish(k)
        pump()
    return order, now


def make_kernel(sizes, unit, rows, experts_here, units):
    nz, nx, ny = sizes
    half_width = 3 * unit + LANES
    wide = unit + LANES
    reduce_widths = ((wide, unit, unit), (unit, wide, unit))
    gather_widths = ((wide, unit, wide), (unit, wide, wide))
    segments = (
        (((0, 0, wide),), ((0, wide, unit),), ((0, wide + unit, unit),)),
        (((0, 0, unit),), ((0, wide, unit), (unit, unit, LANES)), ((0, wide + unit, unit),)),
    )
    per_chunk = nz // HALVES
    spe = CAPACITY * nx * ny
    slots = experts_here * spe
    chunk_rows = per_chunk * spe
    group_tokens = nx * ny * rows
    exchange_bytes = experts_here * 2 * chunk_rows * units * 2
    tasks = build_tasks(sizes, gather_widths, reduce_widths, rows, exchange_bytes)
    order, _ = schedule(tasks)
    gathers = [k for k in tasks if k[0] == "g"]
    reduces = [k for k in tasks if k[0] == "r"]
    number = {k: n for n, k in enumerate(gathers)}
    number.update({k: n for n, k in enumerate(reduces)})
    buffers, buffer_of = {}, {}
    for k in reduces:
        p, c, stage = k[1:4]
        first = ORDERS[c][0]
        shape = []
        for a in sorted(ORDERS[c][:stage]):
            shape.append(sizes[a] // 2 if a == first else sizes[a])
        count = buffers.get((p, c, stage), (0,))[0]
        buffer_of[k] = count
        buffers[(p, c, stage)] = (count + 1,) + tuple(shape) + (rows, reduce_widths[p][c])
    buffer_keys = sorted(buffers)

    def kernel(
        ids_ref, weight_ref, x_ref, lane_hbm, code_hbm, code_t_hbm, gate_hbm, up_hbm, down_hbm,
        out_ref, held01, held2, table_ref, lane_ref, code_ref, code_t_ref, gate_up, down, chosen,
        outs, pre_out, pre_in, fin_in,
        *rest,
    ):
        landing = dict(zip(buffer_keys, rest[: len(buffer_keys)]))
        (constant_sem, own_sem, pair_send, pair_recv, load_sem, load_send, load_recv,
         gather_send, gather_recv, reduce_send, reduce_recv,
         pre_send, pre_recv, fin_send, fin_recv) = rest[len(buffer_keys):]
        z = lax.axis_index("rep")
        e = lax.axis_index("exp")
        core = lax.rem(e, 2)
        chip = lax.div(e, 2)
        y = lax.rem(chip, ny)
        x = lax.div(chip, ny)
        here = (z, x, y)
        partner = (z, e + 1 - 2 * core)

        def held(p, c):
            return held2.at[p] if c == 2 else held01.at[c, p]

        def neighbour(axis, direction):
            moved = list(here)
            moved[axis] = lax.rem(here[axis] + direction + sizes[axis], sizes[axis])
            return (moved[0], (moved[1] * ny + moved[2]) * 2 + core)

        def contract_last(a, b):
            return lax.dot_general(
                a, b, (((1,), (1,)), ((), ())), preferred_element_type=jnp.float32
            )

        barrier = pltpu.get_barrier_semaphore()
        peers = [partner] + [neighbour(a, d) for a in range(3) for d in (1, -1)]
        for peer in peers:
            pl.semaphore_signal(barrier, inc=1, device_id=peer, device_id_type=MESH)

        constants = [
            pltpu.make_async_copy(a, b, constant_sem.at[n])
            for n, (a, b) in enumerate(
                ((lane_hbm, lane_ref), (code_hbm, code_ref), (code_t_hbm, code_t_ref))
            )
        ]
        for copy in constants:
            copy.start()

        experts = LANES // 2
        lane = lax.broadcasted_iota(jnp.int32, (rows, LANES), 1)
        named = jnp.zeros((rows, LANES), jnp.float32)
        weights = jnp.zeros((rows, LANES), jnp.float32)
        below = lax.broadcasted_iota(jnp.int32, (rows, rows), 0)
        across = lax.broadcasted_iota(jnp.int32, (rows, rows), 1)
        same = (across == below).astype(jnp.float32).astype(jnp.bfloat16)
        flipped = [
            contract_last(same, ref[...].astype(jnp.float32).astype(jnp.bfloat16))
            for ref in (ids_ref, weight_ref)
        ]
        for k in range(ids_ref.shape[0]):
            name = flipped[0][:, k:k + 1].astype(jnp.int32)
            named = named + (lane == name).astype(jnp.float32)
            weights = weights + jnp.where(lane == name + experts, flipped[1][:, k:k + 1], 0.0)
        triangle = (across <= below).astype(jnp.bfloat16)
        rank = jnp.dot(triangle, named.astype(jnp.bfloat16), preferred_element_type=jnp.float32)
        table_ref[...] = (named * rank + weights).astype(jnp.bfloat16)

        pl.semaphore_wait(barrier, len(peers))

        def pieces(phase):
            mine = (z, x, y, pl.ds(0, rows))
            return (
                (0, unit, held01.at[(0, phase) + mine + (pl.ds(0, unit),)]),
                (unit, LANES, held01.at[(phase, phase) + mine + (pl.ds(unit, LANES),)]),
                (wide, unit, held01.at[(1, phase) + mine + (pl.ds(0, unit),)]),
                (wide + unit, unit, held2.at[(phase,) + mine + (pl.ds(0, unit),)]),
            )

        table_place = held2.at[core, z, x, y, pl.ds(0, rows), pl.ds(unit, LANES)]
        own_copies, pair_copies = [], []
        for n, (column, width, place) in enumerate(pieces(core)):
            start = pl.multiple_of(core * half_width + column, LANES)
            other = pl.multiple_of((1 - core) * half_width + column, LANES)
            own_copies.append((x_ref.at[:, pl.ds(start, width)], place))
            pair_copies.append((x_ref.at[:, pl.ds(other, width)], place))
        own_copies.append((table_ref, table_place))
        pair_copies.append((table_ref, table_place))
        own_copies = [
            pltpu.make_async_copy(a, b, own_sem.at[n]) for n, (a, b) in enumerate(own_copies)
        ]
        pair_copies = [
            pltpu.make_async_remote_copy(
                src_ref=a, dst_ref=b, send_sem=pair_send.at[n], recv_sem=pair_recv.at[n],
                device_id=partner, device_id_type=MESH,
            )
            for n, (a, b) in enumerate(pair_copies)
        ]
        for copy in pair_copies + own_copies:
            copy.start()

        local = experts_here // 2
        mine_experts = pl.ds(core * local, local)
        loads, sends = [], []
        for n, (source, target) in enumerate(
            (
                (gate_hbm, gate_up.at[mine_experts, 0]),
                (up_hbm, gate_up.at[mine_experts, 1]),
                (down_hbm, down.at[mine_experts]),
            )
        ):
            start = pl.multiple_of(core * half_width, LANES)
            other = pl.multiple_of((1 - core) * half_width, LANES)
            loads.append(
                pltpu.make_async_copy(
                    source.at[:, :, pl.ds(start, half_width)], target, load_sem.at[n]
                )
            )
            sends.append(
                pltpu.make_async_remote_copy(
                    src_ref=source.at[:, :, pl.ds(other, half_width)], dst_ref=target,
                    send_sem=load_send.at[n], recv_sem=load_recv.at[n], device_id=partner,
                    device_id_type=MESH,
                )
            )
        for copy in own_copies + pair_copies:
            copy.wait()
        for copy in loads + sends:
            copy.start()

        def block(p, c, stage, index, half, width):
            axes = ORDERS[c]
            where = []
            for a in range(3):
                if a == axes[stage]:
                    where.append(index)
                elif a in axes[:stage]:
                    if a == axes[0]:
                        where.append(pl.ds(half * (sizes[a] // 2), sizes[a] // 2))
                    else:
                        where.append(pl.ds(0, sizes[a]))
                else:
                    where.append(here[a])
            lead = (p,) if c == 2 else (c, p)
            ref = held2 if c == 2 else held01
            return ref.at[lead + tuple(where) + (pl.ds(0, rows), pl.ds(0, width))]

        def gather_copy(key, received):
            _, p, c, stage, d, s, h = key
            axis = ORDERS[c][stage]
            back = s if received else s - 1
            index = lax.rem(here[axis] - d * back + sizes[axis], sizes[axis])
            place = block(p, c, stage, index, h, gather_widths[p][c])
            n = number[key]
            return pltpu.make_async_remote_copy(
                src_ref=place, dst_ref=place, send_sem=gather_send.at[n],
                recv_sem=gather_recv.at[n], device_id=neighbour(axis, d), device_id_type=MESH,
            )

        def reduce_copy(key):
            _, p, c, stage, d, s, h = key
            axis = ORDERS[c][stage]
            size = sizes[axis]
            index = lax.rem(here[axis] + d * (size // 2 - s + 1) + size, size)
            n = number[key]
            return pltpu.make_async_remote_copy(
                src_ref=block(p, c, stage, index, h, reduce_widths[p][c]),
                dst_ref=landing[(p, c, stage)].at[buffer_of[key]],
                send_sem=reduce_send.at[n], recv_sem=reduce_recv.at[n],
                device_id=neighbour(axis, d), device_id_type=MESH,
            )

        def pre_copy(p, q):
            n = p * HALVES + q
            return pltpu.make_async_remote_copy(
                src_ref=pre_out.at[n], dst_ref=pre_in.at[n], send_sem=pre_send.at[n],
                recv_sem=pre_recv.at[n], device_id=partner, device_id_type=MESH,
            )

        base = chip * experts_here

        def group(p, c, gz, start, width):
            lead = (p,) if c == 2 else (c, p)
            ref = held2 if c == 2 else held01
            value = ref[lead + (gz, slice(None), slice(None), slice(None), pl.ds(start, width))]
            return value.reshape(group_tokens, width)

        def select(p, q, c):
            def one(g, carry):
                gz = q * per_chunk + g
                pick = (lane_ref[...] == base).astype(jnp.bfloat16)
                codes = contract_last(pick, group(p, 2, gz, unit, LANES))
                onehot = (codes == code_ref[...]).astype(jnp.bfloat16)
                for start, column, width in segments[p][c]:
                    picked = jnp.dot(
                        onehot, group(p, c, gz, start, width), preferred_element_type=jnp.float32
                    ).astype(jnp.bfloat16)
                    for n in range(experts_here):
                        chosen[n, pl.ds(pl.multiple_of(g * spe, 16), spe), pl.ds(column, width)] = (
                            picked[n * spe:(n + 1) * spe]
                        )
                return carry

            lax.fori_loop(0, per_chunk, one, 0)

        def project(p, q):
            def one(n, carry):
                for which in range(2):
                    pre_out[p * HALVES + q, n, which] = contract_last(
                        chosen[n], gate_up[n, which]
                    ).astype(jnp.bfloat16)
                return carry

            lax.fori_loop(0, experts_here, one, 0)

        def expand(p, q):
            index = p * HALVES + q

            def one(n, carry):
                values = []
                for which in range(2):
                    mine = pre_out[index, n, which].astype(jnp.float32)
                    values.append(mine + pre_in[index, n, which].astype(jnp.float32))
                hidden = values[0] / (1.0 + jnp.exp(-values[0])) * values[1]
                outcome = jnp.dot(
                    hidden.astype(jnp.bfloat16), down[n], preferred_element_type=jnp.float32
                ).astype(jnp.bfloat16)
                for g in range(per_chunk):
                    outs[g, pl.ds(pl.multiple_of(n * spe, 16), spe)] = (
                        outcome[g * spe:(g + 1) * spe]
                    )
                return carry

            lax.fori_loop(0, experts_here, one, 0)

        def combine(p, q):
            def one(g, carry):
                gz = q * per_chunk + g
                table = group(p, 2, gz, unit, LANES)
                pick = (lane_ref[...] == base).astype(jnp.bfloat16)
                weigh = (lane_ref[...] == base + experts).astype(jnp.bfloat16)
                codes = contract_last(table, pick)
                values = contract_last(table, weigh)
                scatter = jnp.where(codes == code_t_ref[...], values, 0.0).astype(jnp.bfloat16)
                for c in range(3):
                    lead = (p,) if c == 2 else (c, p)
                    ref = held2 if c == 2 else held01
                    for start, column, width in segments[p][c]:
                        summed = jnp.dot(
                            scatter, outs[g, :, pl.ds(column, width)],
                            preferred_element_type=jnp.float32,
                        )
                        where = lead + (gz, slice(None), slice(None), slice(None))
                        ref[where + (pl.ds(start, width),)] = summed.astype(jnp.bfloat16).reshape(
                            nx, ny, rows, width
                        )
                return carry

            lax.fori_loop(0, per_chunk, one, 0)

        def add_into(target, sources):
            lead = target.shape[:-2]

            def one_block(where):
                total = target[where].astype(jnp.float32)
                for source in sources:
                    total = total + source[where].astype(jnp.float32)
                target[where] = total.astype(jnp.bfloat16)

            if not lead:
                one_block(...)
                return

            def one(n, carry):
                if len(lead) == 1:
                    one_block((n,))
                else:
                    for m in range(lead[1]):
                        one_block((n, m))
                return carry

            lax.fori_loop(0, lead[0], one, 0)

        arrived = set()

        def reduce_arrival(key):
            reduce_copy(key).wait_recv()
            arrived.add(key)
            _, p, c, stage, d, s, h = key
            axis = ORDERS[c][stage]
            size = sizes[axis]
            last = size // 2
            width = reduce_widths[p][c]
            if s < last:
                index = lax.rem(here[axis] + d * (last - s) + size, size)
                add_into(
                    block(p, c, stage, index, h, width),
                    [landing[(p, c, stage)].at[buffer_of[key]]],
                )
                return
            parts = [k for k in reduces if k[:4] == key[:4] and k[5] == last and k[6] == h]
            if all(k in arrived for k in parts):
                add_into(
                    block(p, c, stage, here[axis], h, width),
                    [landing[(p, c, stage)].at[buffer_of[k]] for k in parts],
                )

        loaded = set()
        for kind, key in order:
            if kind == "start":
                if key[0] == "g":
                    gather_copy(key, False).start()
                elif key[0] == "r":
                    reduce_copy(key).start()
                else:
                    pre_copy(key[1], key[2]).start()
            elif kind == "arrive":
                if key[0] == "g":
                    gather_copy(key, True).wait_recv()
                elif key[0] == "r":
                    reduce_arrival(key)
                else:
                    pre_copy(key[1], key[2]).wait_recv()
            elif key[0] == "select":
                if "constants" not in loaded:
                    loaded.add("constants")
                    for copy in constants:
                        copy.wait()
                select(*key[1:])
            elif key[0] == "project":
                if "weights" not in loaded:
                    loaded.add("weights")
                    for copy in loads + sends:
                        copy.wait()
                project(*key[1:])
            elif key[0] == "expand":
                expand(*key[1:])
            else:
                if key[2] == 0:
                    for k in gathers:
                        if k[1] == key[1]:
                            gather_copy(k, False).wait_send()
                combine(*key[1:])

        last_copies = [
            pltpu.make_async_remote_copy(
                src_ref=place, dst_ref=fin_in.at[:, pl.ds(column, width)], send_sem=fin_send.at[n],
                recv_sem=fin_recv.at[n], device_id=partner, device_id_type=MESH,
            )
            for n, (column, width, place) in enumerate(pieces(1 - core))
        ]
        for copy in last_copies:
            copy.start()
        for column, width, place in pieces(core):
            start = pl.multiple_of(core * half_width + column, LANES)
            out_ref[:, pl.ds(start, width)] = place[...]
        for k in reduces:
            reduce_copy(k).wait_send()
        for p in range(PHASES):
            for q in range(HALVES):
                pre_copy(p, q).wait_send()
        for copy in last_copies:
            copy.wait()
        out_ref[:, pl.ds(pl.multiple_of((1 - core) * half_width, LANES), half_width)] = fin_in[...]

    bf16 = jnp.bfloat16
    dma = pltpu.SemaphoreType.DMA
    chunks = PHASES * HALVES
    pre_shape = (chunks, experts_here, 2, chunk_rows, units)
    scratch = [
        pltpu.VMEM((2, PHASES, nz, nx, ny, rows, wide), bf16),
        pltpu.VMEM((PHASES, nz, nx, ny, rows, wide), bf16),
        pltpu.VMEM((rows, LANES), bf16),
        pltpu.VMEM((slots, LANES), jnp.int32),
        pltpu.VMEM((slots, group_tokens), jnp.float32),
        pltpu.VMEM((group_tokens, slots), jnp.float32),
        pltpu.VMEM((experts_here, 2, units, half_width), bf16),
        pltpu.VMEM((experts_here, units, half_width), bf16),
        pltpu.VMEM((experts_here, chunk_rows, half_width), bf16),
        pltpu.VMEM((per_chunk, slots, half_width), bf16),
        pltpu.VMEM(pre_shape, bf16),
        pltpu.VMEM(pre_shape, bf16),
        pltpu.VMEM((rows, half_width), bf16),
        *[pltpu.VMEM(buffers[k], bf16) for k in buffer_keys],
        dma((3,)), dma((5,)), dma((5,)), dma((5,)), dma((3,)), dma((3,)), dma((3,)),
        dma((len(gathers),)), dma((len(gathers),)), dma((len(reduces),)), dma((len(reduces),)),
        dma((chunks,)), dma((chunks,)), dma((4,)), dma((4,)),
    ]
    slot = np.arange(slots)
    token = np.arange(group_tokens)
    lane_constant = (np.arange(LANES)[None, :] - (slot // spe)[:, None]).astype(np.int32)
    same = (slot % spe // CAPACITY)[:, None] == (token // rows)[None, :]
    code = np.where(same, (slot % CAPACITY + 1)[:, None], -1).astype(np.float32)
    return kernel, scratch, (lane_constant, code, np.ascontiguousarray(code.T))


def solution(mesh):
    nz = mesh.shape["rep"]
    nx = int(round((mesh.shape["exp"] // 2) ** 0.5))
    ny = mesh.shape["exp"] // 2 // nx

    def on_device(tokens, routed_experts, route_weights, gate_weight, up_weight, down_weight):
        rows, width = tokens.shape
        local, units = gate_weight.shape[:2]
        unit = (width // 2 // LANES - 1) // 3 * LANES
        kernel, scratch, constants = make_kernel((nz, nx, ny), unit, rows, 2 * local, units)
        vmem = pl.BlockSpec(memory_space=pltpu.VMEM)
        hbm = pl.BlockSpec(memory_space=pl.ANY)
        return pl.pallas_call(
            kernel,
            out_shape=jax.ShapeDtypeStruct((rows, width), jnp.bfloat16),
            in_specs=[vmem] * 2 + [hbm] * 7,
            out_specs=vmem,
            scratch_shapes=scratch,
            compiler_params=pltpu.CompilerParams(
                collective_id=0, has_side_effects=True, vmem_limit_bytes=67_000_000
            ),
        )(
            routed_experts.T, route_weights.T, tokens, *constants, gate_weight, up_weight,
            down_weight,
        )

    placed = (
        P(("rep", "exp"), None),
        P(("rep", "exp"), None),
        P(("rep", "exp"), None),
        P("exp", "rep", None),
        P("exp", "rep", None),
        P("exp", "rep", None),
    )
    return jax.shard_map(
        on_device, mesh=mesh, in_specs=placed, out_specs=P(("rep", "exp"), None), check_vma=False
    )
```

```python
import heapq

import jax
import jax.numpy as jnp
import numpy as np
from jax import lax
from jax.experimental import pallas as pl
from jax.experimental.pallas import tpu as pltpu
from jax.sharding import PartitionSpec as P

MESH = pl.DeviceIdType.MESH
LANES = 128
CAPACITY = 3
PHASES = 2
HALVES = 2
ORDERS = ((0, 1, 2), (0, 2, 1), (1, 2, 0))
LONG = (1, -1, 1)
RATE = 46000.0
PAIR_RATE = 150000.0
LATENCY = 1.8
LOOK = 2.0
ADD_RATE = 1.5e6
COSTS = {"select": 0.8, "fetch": 0.3, "pick": 0.3, "project": 2.5, "expand": 1.9, "combine": 1.2, "spread": 0.3}


def steps_of(size, split, long, gathering):
    middle = size // 2
    odd_step = middle if gathering else 1
    found = []
    for step in range(1, middle + 1):
        for direction in (1, -1):
            if split:
                first = 0 if direction == 1 else 1
                both = (first, 1 - first) if gathering else (1 - first, first)
                for half in both:
                    if step != odd_step or half == first:
                        found.append((direction, step, half))
            elif step != odd_step or direction == long:
                found.append((direction, step, 0))
    return found


def block_bytes(sizes, width, rows, order, stage, slots):
    total = rows * width * 2
    if order[2] == 0 and stage == 2:
        return slots * width
    for axis in order[:stage]:
        total *= sizes[axis]
    return total // 2 if stage else total


def build_tasks(sizes, gather_widths, reduce_widths, rows, exchange_bytes, slots):
    tasks = {}
    chunk_before = None
    for p in range(PHASES):
        arrivals = {}
        for c, order in enumerate(ORDERS):
            for stage in range(3):
                axis = order[stage]
                for d, s, h in steps_of(sizes[axis], stage > 0, LONG[c], True):
                    if s > 1:
                        needs = {("g", p, c, stage, d, s - 1, h)}
                    elif stage == 0:
                        needs = set()
                    elif c == 2 and stage == 2:
                        needs = {("pick", p)}
                    else:
                        needs = {
                            k for k in tasks
                            if k[:4] == ("g", p, c, stage - 1) and (stage == 1 or k[6] == h)
                        }
                    key = ("g", p, c, stage, d, s, h)
                    width = reduce_widths[c] if stage == 2 else gather_widths[c]
                    size = block_bytes(sizes, width, rows, order, stage, slots)
                    tasks[key] = ((axis, d), size, needs)
                if c == 2 and stage == 1:
                    plane = {k for k in tasks if k[:4] == ("g", p, 2, 1)}
                    tasks[("pick", p)] = (None, COSTS["pick"], plane)
                    size = sizes[1] * sizes[2] * rows * LANES * 2
                    for d, s, h in steps_of(sizes[0], False, -1, True):
                        needs = {("t", p, 3, 2, d, s - 1, h)} if s > 1 else {("pick", p)}
                        tasks[("t", p, 3, 2, d, s, h)] = ((0, d), size, needs)
                    arrivals[3] = {k for k in tasks if k[:2] == ("t", p)}
            arrivals[c] = {k for k in tasks if k[:4] == ("g", p, c, 2)}
        for q in range(HALVES):
            for c in range(3):
                if c < 2:
                    needs = arrivals[3] | {k for k in arrivals[c] if k[6] == q}
                else:
                    needs = set(arrivals[2])
                if chunk_before is not None:
                    needs.add(("project",) + chunk_before)
                cost = COSTS["select"] if c < 2 else COSTS["fetch"]
                tasks[("select", p, q, c)] = (None, cost, needs)
            tasks[("project", p, q)] = (
                None, COSTS["project"], {("select", p, q, c) for c in range(3)}
            )
            tasks[("x", p, q)] = (("pair", 0), exchange_bytes, {("project", p, q)})
            needs = {("x", p, q)}
            if chunk_before is not None:
                needs.add(("combine",) + chunk_before)
            tasks[("expand", p, q)] = (None, COSTS["expand"], needs)
            tasks[("combine", p, q)] = (None, COSTS["combine"], {("expand", p, q)})
            chunk_before = (p, q)
        tasks[("spread", p)] = (None, COSTS["spread"], set())
        for c, order in enumerate(ORDERS):
            for stage in (2, 1, 0):
                axis = order[stage]
                steps = steps_of(sizes[axis], stage > 0, LONG[c], False)
                for d, s, h in steps:
                    if (d, s - 1, h) in steps:
                        needs = {("r", p, c, stage, d, s - 1, h)}
                    elif stage == 2 and c == 2:
                        needs = {("expand", p, q) for q in range(HALVES)}
                    elif stage == 2:
                        needs = {("combine", p, h)}
                    elif stage == 1 and c == 2:
                        needs = {("spread", p)}
                    else:
                        needs = {
                            k for k in tasks
                            if k[:4] == ("r", p, c, stage + 1)
                            and k[5] == sizes[order[stage + 1]] // 2
                            and (stage == 0 or k[6] == h)
                        }
                    key = ("r", p, c, stage, d, s, h)
                    size = block_bytes(sizes, reduce_widths[c], rows, order, stage, slots)
                    tasks[key] = ((axis, d), size, needs)
                    if c == 2 and stage == 2 and s == sizes[0] // 2:
                        tasks[("spread", p)][2].add(key)
    return tasks


def priority(key):
    if key[0] in "gt":
        return key[1] * 10 + key[3]
    if key[0] == "r":
        return 20 + key[1] * 10 + key[3]
    first = {"pick": -10, "spread": -10, "x": 0, "expand": 10, "combine": 10}
    return key[1] + first.get(key[0], 40)


def schedule(tasks):
    waiting = {k: set(v[2]) for k, v in tasks.items()}
    readers = {}
    for k, v in tasks.items():
        for other in v[2]:
            readers.setdefault(other, []).append(k)
    place = {k: n for n, k in enumerate(tasks)}
    free, pending, arriving, computing, order = {}, {}, [], [], []
    now = 0.0

    def ready(k):
        link = tasks[k][0]
        queue = computing if link is None else pending.setdefault(link, [])
        heapq.heappush(queue, (priority(k), place[k], k))

    def pump():
        for link, queue in pending.items():
            while queue and free.get(link, 0.0) - now < LOOK:
                k = heapq.heappop(queue)[2]
                order.append(("start", k))
                rate = PAIR_RATE if link[0] == "pair" else RATE
                free[link] = max(now, free.get(link, 0.0)) + tasks[k][1] / rate
                heapq.heappush(arriving, (free[link] + LATENCY, place[k], k))

    def finish(k):
        for reader in readers.get(k, ()):
            waiting[reader].discard(k)
            if not waiting[reader]:
                ready(reader)

    for k in tasks:
        if not waiting[k]:
            ready(k)
    pump()
    while arriving or computing:
        if arriving and (arriving[0][0] <= now or not computing):
            when, _, k = heapq.heappop(arriving)
            now = max(now, when) + 0.03
            if k[0] == "r":
                now += tasks[k][1] / ADD_RATE
            order.append(("arrive", k))
        else:
            k = heapq.heappop(computing)[2]
            now += tasks[k][1]
            order.append(("compute", k))
        finish(k)
        pump()
    return order, now


def make_kernel(sizes, widths, rows, experts_here, units):
    nz, nx, ny = sizes
    half_width = sum(widths)
    offsets = (0, widths[0], widths[0] + widths[1])
    gather_widths = (widths[0], widths[1], widths[2] + LANES)
    per_chunk = nz // HALVES
    spe = CAPACITY * nx * ny
    slots = experts_here * spe
    chunk_rows = per_chunk * spe
    group_tokens = nx * ny * rows
    exchange_bytes = experts_here * 2 * chunk_rows * units * 2
    tasks = build_tasks(sizes, gather_widths, widths, rows, exchange_bytes, slots)
    order, _ = schedule(tasks)
    gathers = [k for k in tasks if k[0] in "gt"]
    reduces = [k for k in tasks if k[0] == "r"]
    number = {k: n for n, k in enumerate(gathers)}
    number.update({k: n for n, k in enumerate(reduces)})
    buffers, buffer_of = {}, {}
    for k in reduces:
        p, c, stage = k[1:4]
        first = ORDERS[c][0]
        shape = []
        for a in sorted(ORDERS[c][:stage]):
            shape.append(sizes[a] // 2 if a == first else sizes[a])
        count = buffers.get((p, c, stage), (0,))[0]
        buffer_of[k] = count
        if c == 2 and stage == 2:
            buffers[(p, c, stage)] = (count + 1, slots // 2, widths[c])
        else:
            buffers[(p, c, stage)] = (count + 1,) + tuple(shape) + (rows, widths[c])
    buffer_keys = sorted(buffers)

    def kernel(
        ids_ref, weight_ref, x_ref, lane_hbm, code_hbm, code_t_hbm, gate_hbm, up_hbm, down_hbm,
        out_ref, held01, plane, slotted, tables, table_ref, lane_ref, code_ref, code_t_ref, gate_up, down, chosen,
        outs, pre_out, pre_in, fin_in,
        *rest,
    ):
        landing = dict(zip(buffer_keys, rest[: len(buffer_keys)]))
        (constant_sem, own_sem, pair_send, pair_recv, load_sem, load_send, load_recv,
         gather_send, gather_recv, reduce_send, reduce_recv,
         pre_send, pre_recv, fin_send, fin_recv) = rest[len(buffer_keys):]
        z = lax.axis_index("rep")
        e = lax.axis_index("exp")
        core = lax.rem(e, 2)
        chip = lax.div(e, 2)
        y = lax.rem(chip, ny)
        x = lax.div(chip, ny)
        here = (z, x, y)
        partner = (z, e + 1 - 2 * core)

        def neighbour(axis, direction):
            moved = list(here)
            moved[axis] = lax.rem(here[axis] + direction + sizes[axis], sizes[axis])
            return (moved[0], (moved[1] * ny + moved[2]) * 2 + core)

        def contract_last(a, b):
            return lax.dot_general(
                a, b, (((1,), (1,)), ((), ())), preferred_element_type=jnp.float32
            )

        barrier = pltpu.get_barrier_semaphore()
        peers = [partner] + [neighbour(a, d) for a in range(3) for d in (1, -1)]
        for peer in peers:
            pl.semaphore_signal(barrier, inc=1, device_id=peer, device_id_type=MESH)

        constants = [
            pltpu.make_async_copy(a, b, constant_sem.at[n])
            for n, (a, b) in enumerate(
                ((lane_hbm, lane_ref), (code_hbm, code_ref), (code_t_hbm, code_t_ref))
            )
        ]
        for copy in constants:
            copy.start()

        experts = LANES // 2
        lane = lax.broadcasted_iota(jnp.int32, (rows, LANES), 1)
        named = jnp.zeros((rows, LANES), jnp.float32)
        weights = jnp.zeros((rows, LANES), jnp.float32)
        below = lax.broadcasted_iota(jnp.int32, (rows, rows), 0)
        across = lax.broadcasted_iota(jnp.int32, (rows, rows), 1)
        same = (across == below).astype(jnp.float32).astype(jnp.bfloat16)
        flipped = [
            contract_last(same, ref[...].astype(jnp.float32).astype(jnp.bfloat16))
            for ref in (ids_ref, weight_ref)
        ]
        for k in range(ids_ref.shape[0]):
            name = flipped[0][:, k:k + 1].astype(jnp.int32)
            named = named + (lane == name).astype(jnp.float32)
            weights = weights + jnp.where(lane == name + experts, flipped[1][:, k:k + 1], 0.0)
        triangle = (across <= below).astype(jnp.bfloat16)
        rank = jnp.dot(triangle, named.astype(jnp.bfloat16), preferred_element_type=jnp.float32)
        table_ref[...] = (named * rank + weights).astype(jnp.bfloat16)

        pl.semaphore_wait(barrier, len(peers))

        def pieces(phase):
            mine = (z, x, y, pl.ds(0, rows))
            return (
                (offsets[0], widths[0], held01.at[(0, phase) + mine + (pl.ds(0, widths[0]),)]),
                (offsets[1], widths[1], held01.at[(1, phase) + mine + (pl.ds(0, widths[1]),)]),
                (offsets[2], widths[2], plane.at[phase, x, y, pl.ds(0, rows), pl.ds(0, widths[2])]),
            )

        table_place = plane.at[core, x, y, pl.ds(0, rows), pl.ds(widths[2], LANES)]
        own_copies, pair_copies = [], []
        for n, (column, width, place) in enumerate(pieces(core)):
            start = pl.multiple_of(core * half_width + column, LANES)
            other = pl.multiple_of((1 - core) * half_width + column, LANES)
            own_copies.append((x_ref.at[:, pl.ds(start, width)], place))
            pair_copies.append((x_ref.at[:, pl.ds(other, width)], place))
        own_copies.append((table_ref, table_place))
        pair_copies.append((table_ref, table_place))
        own_copies = [
            pltpu.make_async_copy(a, b, own_sem.at[n]) for n, (a, b) in enumerate(own_copies)
        ]
        pair_copies = [
            pltpu.make_async_remote_copy(
                src_ref=a, dst_ref=b, send_sem=pair_send.at[n], recv_sem=pair_recv.at[n],
                device_id=partner, device_id_type=MESH,
            )
            for n, (a, b) in enumerate(pair_copies)
        ]
        for copy in pair_copies + own_copies:
            copy.start()

        local = experts_here // 2
        mine_experts = pl.ds(core * local, local)
        loads, sends = [], []
        for n, (source, target) in enumerate(
            (
                (gate_hbm, gate_up.at[mine_experts, 0]),
                (up_hbm, gate_up.at[mine_experts, 1]),
                (down_hbm, down.at[mine_experts]),
            )
        ):
            start = pl.multiple_of(core * half_width, LANES)
            other = pl.multiple_of((1 - core) * half_width, LANES)
            loads.append(
                pltpu.make_async_copy(
                    source.at[:, :, pl.ds(start, half_width)], target, load_sem.at[n]
                )
            )
            sends.append(
                pltpu.make_async_remote_copy(
                    src_ref=source.at[:, :, pl.ds(other, half_width)], dst_ref=target,
                    send_sem=load_send.at[n], recv_sem=load_recv.at[n], device_id=partner,
                    device_id_type=MESH,
                )
            )
        for copy in own_copies + pair_copies:
            copy.wait()
        for copy in loads + sends:
            copy.start()

        def block(p, c, stage, index, half, width):
            if c == 3:
                return tables.at[p, index]
            if c == 2 and stage == 2:
                part = slots // 2
                return slotted.at[p, index, pl.ds(half * part, part)]
            axes = ORDERS[c]
            where = []
            for a in range(3):
                if a == axes[stage]:
                    where.append(index)
                elif a in axes[:stage]:
                    if a == axes[0]:
                        where.append(pl.ds(half * (sizes[a] // 2), sizes[a] // 2))
                    else:
                        where.append(pl.ds(0, sizes[a]))
                else:
                    where.append(here[a])
            if c == 2:
                return plane.at[(p,) + tuple(where[1:]) + (pl.ds(0, rows), pl.ds(0, width))]
            return held01.at[(c, p) + tuple(where) + (pl.ds(0, rows), pl.ds(0, width))]

        def gather_copy(key, received):
            _, p, c, stage, d, s, h = key
            axis = ORDERS[c][stage] if c < 3 else 0
            back = s if received else s - 1
            index = lax.rem(here[axis] - d * back + sizes[axis], sizes[axis])
            place = block(p, c, stage, index, h, gather_widths[c] if c < 3 else LANES)
            n = number[key]
            return pltpu.make_async_remote_copy(
                src_ref=place, dst_ref=place, send_sem=gather_send.at[n],
                recv_sem=gather_recv.at[n], device_id=neighbour(axis, d), device_id_type=MESH,
            )

        def reduce_copy(key):
            _, p, c, stage, d, s, h = key
            axis = ORDERS[c][stage]
            size = sizes[axis]
            index = lax.rem(here[axis] + d * (size // 2 - s + 1) + size, size)
            n = number[key]
            return pltpu.make_async_remote_copy(
                src_ref=block(p, c, stage, index, h, widths[c]),
                dst_ref=landing[(p, c, stage)].at[buffer_of[key]],
                send_sem=reduce_send.at[n], recv_sem=reduce_recv.at[n],
                device_id=neighbour(axis, d), device_id_type=MESH,
            )

        def pre_copy(p, q):
            n = p * HALVES + q
            return pltpu.make_async_remote_copy(
                src_ref=pre_out.at[n], dst_ref=pre_in.at[n], send_sem=pre_send.at[n],
                recv_sem=pre_recv.at[n], device_id=partner, device_id_type=MESH,
            )

        base = chip * experts_here

        def table_of(p, gz):
            return tables[p, gz].reshape(group_tokens, LANES)

        def onehot_of(table):
            wanted = (lane_ref[...] == base).astype(jnp.bfloat16)
            return (contract_last(wanted, table) == code_ref[...]).astype(jnp.bfloat16)

        def scatter_of(table):
            wanted = (lane_ref[...] == base).astype(jnp.bfloat16)
            weigh = (lane_ref[...] == base + experts).astype(jnp.bfloat16)
            codes = contract_last(table, wanted)
            values = contract_last(table, weigh)
            return jnp.where(codes == code_t_ref[...], values, 0.0).astype(jnp.bfloat16)

        def pick_rows(p):
            tables[p, z] = plane[p, :, :, :, pl.ds(widths[2], LANES)]
            value = plane[p, :, :, :, pl.ds(0, widths[2])].reshape(group_tokens, widths[2])
            slotted[p, z] = jnp.dot(
                onehot_of(table_of(p, z)), value, preferred_element_type=jnp.float32
            ).astype(jnp.bfloat16)

        def spread(p):
            plane[p, :, :, :, pl.ds(0, widths[2])] = jnp.dot(
                scatter_of(table_of(p, z)), slotted[p, z], preferred_element_type=jnp.float32
            ).astype(jnp.bfloat16).reshape(nx, ny, rows, widths[2])

        def select(p, q, c):
            columns = pl.ds(offsets[c], widths[c])

            def one(g, carry):
                gz = q * per_chunk + g
                if c == 2:
                    picked = slotted[p, gz]
                else:
                    value = held01[c, p, gz].reshape(group_tokens, widths[c])
                    picked = jnp.dot(
                        onehot_of(table_of(p, gz)), value, preferred_element_type=jnp.float32
                    ).astype(jnp.bfloat16)
                for n in range(experts_here):
                    chosen[n, pl.ds(pl.multiple_of(g * spe, 16), spe), columns] = (
                        picked[n * spe:(n + 1) * spe]
                    )
                return carry

            lax.fori_loop(0, per_chunk, one, 0)

        def project(p, q):
            def one(n, carry):
                for which in range(2):
                    pre_out[p * HALVES + q, n, which] = contract_last(
                        chosen[n], gate_up[n, which]
                    ).astype(jnp.bfloat16)
                return carry

            lax.fori_loop(0, experts_here, one, 0)

        def expand(p, q):
            index = p * HALVES + q

            def one(n, carry):
                values = []
                for which in range(2):
                    mine = pre_out[index, n, which].astype(jnp.float32)
                    values.append(mine + pre_in[index, n, which].astype(jnp.float32))
                hidden = values[0] / (1.0 + jnp.exp(-values[0])) * values[1]
                outcome = jnp.dot(
                    hidden.astype(jnp.bfloat16), down[n], preferred_element_type=jnp.float32
                ).astype(jnp.bfloat16)
                for g in range(per_chunk):
                    place = pl.ds(pl.multiple_of(n * spe, 16), spe)
                    part = outcome[g * spe:(g + 1) * spe]
                    outs[g, place] = part[:, :offsets[2]]
                    slotted[p, q * per_chunk + g, place] = part[:, offsets[2]:]
                return carry

            lax.fori_loop(0, experts_here, one, 0)

        def combine(p, q):
            def one(g, carry):
                gz = q * per_chunk + g
                scatter = scatter_of(table_of(p, gz))
                for c in range(2):
                    held01[c, p, gz] = jnp.dot(
                        scatter, outs[g, :, pl.ds(offsets[c], widths[c])],
                        preferred_element_type=jnp.float32,
                    ).astype(jnp.bfloat16).reshape(nx, ny, rows, widths[c])
                return carry

            lax.fori_loop(0, per_chunk, one, 0)

        def add_into(target, sources):
            lead = target.shape[:-2]

            def one_block(where):
                total = target[where].astype(jnp.float32)
                for source in sources:
                    total = total + source[where].astype(jnp.float32)
                target[where] = total.astype(jnp.bfloat16)

            if not lead:
                one_block(...)
                return

            def one(n, carry):
                if len(lead) == 1:
                    one_block((n,))
                else:
                    for m in range(lead[1]):
                        one_block((n, m))
                return carry

            lax.fori_loop(0, lead[0], one, 0)

        arrived = set()

        def reduce_arrival(key):
            reduce_copy(key).wait_recv()
            arrived.add(key)
            _, p, c, stage, d, s, h = key
            axis = ORDERS[c][stage]
            size = sizes[axis]
            last = size // 2
            width = widths[c]
            if s < last:
                index = lax.rem(here[axis] + d * (last - s) + size, size)
                add_into(
                    block(p, c, stage, index, h, width),
                    [landing[(p, c, stage)].at[buffer_of[key]]],
                )
                return
            parts = [k for k in reduces if k[:4] == key[:4] and k[5] == last and k[6] == h]
            if all(k in arrived for k in parts):
                add_into(
                    block(p, c, stage, here[axis], h, width),
                    [landing[(p, c, stage)].at[buffer_of[k]] for k in parts],
                )

        loaded = set()
        for kind, key in order:
            if kind == "start":
                if key[0] in "gt":
                    gather_copy(key, False).start()
                elif key[0] == "r":
                    reduce_copy(key).start()
                else:
                    pre_copy(key[1], key[2]).start()
            elif kind == "arrive":
                if key[0] in "gt":
                    gather_copy(key, True).wait_recv()
                elif key[0] == "r":
                    reduce_arrival(key)
                else:
                    pre_copy(key[1], key[2]).wait_recv()
            elif key[0] == "pick":
                if "constants" not in loaded:
                    loaded.add("constants")
                    for copy in constants:
                        copy.wait()
                pick_rows(key[1])
            elif key[0] == "spread":
                spread(key[1])
            elif key[0] == "select":
                select(*key[1:])
            elif key[0] == "project":
                if "weights" not in loaded:
                    loaded.add("weights")
                    for copy in loads + sends:
                        copy.wait()
                project(*key[1:])
            elif key[0] == "expand":
                if key[2] == 0:
                    for k in gathers:
                        if k[1] == key[1]:
                            gather_copy(k, False).wait_send()
                expand(*key[1:])
            else:
                combine(*key[1:])

        last_copies = [
            pltpu.make_async_remote_copy(
                src_ref=place, dst_ref=fin_in.at[:, pl.ds(column, width)], send_sem=fin_send.at[n],
                recv_sem=fin_recv.at[n], device_id=partner, device_id_type=MESH,
            )
            for n, (column, width, place) in enumerate(pieces(1 - core))
        ]
        for copy in last_copies:
            copy.start()
        for column, width, place in pieces(core):
            start = pl.multiple_of(core * half_width + column, LANES)
            out_ref[:, pl.ds(start, width)] = place[...]
        for k in reduces:
            reduce_copy(k).wait_send()
        for p in range(PHASES):
            for q in range(HALVES):
                pre_copy(p, q).wait_send()
        for copy in last_copies:
            copy.wait()
        out_ref[:, pl.ds(pl.multiple_of((1 - core) * half_width, LANES), half_width)] = fin_in[...]

    bf16 = jnp.bfloat16
    dma = pltpu.SemaphoreType.DMA
    chunks = PHASES * HALVES
    pre_shape = (chunks, experts_here, 2, chunk_rows, units)
    scratch = [
        pltpu.VMEM((2, PHASES, nz, nx, ny, rows, widths[0]), bf16),
        pltpu.VMEM((PHASES, nx, ny, rows, widths[2] + LANES), bf16),
        pltpu.VMEM((PHASES, nz, slots, widths[2]), bf16),
        pltpu.VMEM((PHASES, nz, nx, ny, rows, LANES), bf16),
        pltpu.VMEM((rows, LANES), bf16),
        pltpu.VMEM((slots, LANES), jnp.int32),
        pltpu.VMEM((slots, group_tokens), jnp.float32),
        pltpu.VMEM((group_tokens, slots), jnp.float32),
        pltpu.VMEM((experts_here, 2, units, half_width), bf16),
        pltpu.VMEM((experts_here, units, half_width), bf16),
        pltpu.VMEM((experts_here, chunk_rows, half_width), bf16),
        pltpu.VMEM((per_chunk, slots, offsets[2]), bf16),
        pltpu.VMEM(pre_shape, bf16),
        pltpu.VMEM(pre_shape, bf16),
        pltpu.VMEM((rows, half_width), bf16),
        *[pltpu.VMEM(buffers[k], bf16) for k in buffer_keys],
        dma((3,)), dma((4,)), dma((4,)), dma((4,)), dma((3,)), dma((3,)), dma((3,)),
        dma((len(gathers),)), dma((len(gathers),)), dma((len(reduces),)), dma((len(reduces),)),
        dma((chunks,)), dma((chunks,)), dma((3,)), dma((3,)),
    ]
    slot = np.arange(slots)
    token = np.arange(group_tokens)
    lane_constant = (np.arange(LANES)[None, :] - (slot // spe)[:, None]).astype(np.int32)
    same = (slot % spe // CAPACITY)[:, None] == (token // rows)[None, :]
    code = np.where(same, (slot % CAPACITY + 1)[:, None], -1).astype(np.float32)
    return kernel, scratch, (lane_constant, code, np.ascontiguousarray(code.T))


def solution(mesh):
    nz = mesh.shape["rep"]
    nx = int(round((mesh.shape["exp"] // 2) ** 0.5))
    ny = mesh.shape["exp"] // 2 // nx

    def on_device(tokens, routed_experts, route_weights, gate_weight, up_weight, down_weight):
        rows, width = tokens.shape
        local, units = gate_weight.shape[:2]
        thin = max(1, 5 * (width // 2 // LANES) // 16) * LANES
        widths = (thin, thin, width // 2 - 2 * thin)
        kernel, scratch, constants = make_kernel((nz, nx, ny), widths, rows, 2 * local, units)
        vmem = pl.BlockSpec(memory_space=pltpu.VMEM)
        hbm = pl.BlockSpec(memory_space=pl.ANY)
        return pl.pallas_call(
            kernel,
            out_shape=jax.ShapeDtypeStruct((rows, width), jnp.bfloat16),
            in_specs=[vmem] * 2 + [hbm] * 7,
            out_specs=vmem,
            scratch_shapes=scratch,
            compiler_params=pltpu.CompilerParams(
                collective_id=0, has_side_effects=True, vmem_limit_bytes=67_000_000
            ),
        )(
            routed_experts.T, route_weights.T, tokens, *constants, gate_weight, up_weight,
            down_weight,
        )

    placed = (
        P(("rep", "exp"), None),
        P(("rep", "exp"), None),
        P(("rep", "exp"), None),
        P("exp", "rep", None),
        P("exp", "rep", None),
        P("exp", "rep", None),
    )
    return jax.shard_map(
        on_device, mesh=mesh, in_specs=placed, out_specs=P(("rep", "exp"), None), check_vma=False
    )
```

```python
import heapq

import jax
import jax.numpy as jnp
import numpy as np
from jax import lax
from jax.experimental import pallas as pl
from jax.experimental.pallas import tpu as pltpu
from jax.sharding import PartitionSpec as P

MESH = pl.DeviceIdType.MESH
LANES = 128
CAPACITY = 3
PHASES = 2
HALVES = 2
ORDERS = ((0, 1, 2), (0, 2, 1), (1, 2, 0))
LONG = (1, -1, 1)
RATE = 46000.0
PAIR_RATE = 150000.0
LATENCY = 3.0
LOOK = 2.0
ADD_RATE = 1.5e6
COSTS = {"select": 0.8, "fetch": 0.3, "pick": 0.3, "project": 2.5, "expand": 1.9, "combine": 1.2, "spread": 0.3}


def steps_of(size, split, long, gathering):
    middle = size // 2
    odd_step = middle if gathering else 1
    found = []
    for step in range(1, middle + 1):
        for direction in (1, -1):
            if split:
                first = 0 if direction == 1 else 1
                both = (first, 1 - first) if gathering else (1 - first, first)
                for half in both:
                    if step != odd_step or half == first:
                        found.append((direction, step, half))
            elif step != odd_step or direction == long:
                found.append((direction, step, 0))
    return found


def block_bytes(sizes, width, rows, order, stage, slots):
    total = rows * width * 2
    if order[2] == 0 and stage == 2:
        return slots * width
    for axis in order[:stage]:
        total *= sizes[axis]
    return total // 2 if stage else total


def build_tasks(sizes, gather_widths, reduce_widths, rows, exchange_bytes, slots):
    tasks = {}
    chunk_before = None
    for p in range(PHASES):
        arrivals = {}
        for c, order in enumerate(ORDERS):
            for stage in range(3):
                axis = order[stage]
                for d, s, h in steps_of(sizes[axis], stage > 0, LONG[c], True):
                    if s > 1:
                        needs = {("g", p, c, stage, d, s - 1, h)}
                    elif stage == 0:
                        needs = set()
                    elif c == 2 and stage == 2:
                        needs = {("pick", p)}
                    else:
                        needs = {
                            k for k in tasks
                            if k[:4] == ("g", p, c, stage - 1) and (stage == 1 or k[6] == h)
                        }
                    key = ("g", p, c, stage, d, s, h)
                    width = reduce_widths[c] if stage == 2 else gather_widths[c]
                    size = block_bytes(sizes, width, rows, order, stage, slots)
                    tasks[key] = ((axis, d), size, needs)
                if c == 2 and stage == 1:
                    plane = {k for k in tasks if k[:4] == ("g", p, 2, 1)}
                    tasks[("pick", p)] = (None, COSTS["pick"], plane)
                    size = sizes[1] * sizes[2] * rows * LANES * 2
                    for d, s, h in steps_of(sizes[0], False, -1, True):
                        needs = {("t", p, 3, 2, d, s - 1, h)} if s > 1 else {("pick", p)}
                        tasks[("t", p, 3, 2, d, s, h)] = ((0, d), size, needs)
                    arrivals[3] = {k for k in tasks if k[:2] == ("t", p)}
            arrivals[c] = {k for k in tasks if k[:4] == ("g", p, c, 2)}
        for q in range(HALVES):
            for c in range(3):
                if c < 2:
                    needs = arrivals[3] | {k for k in arrivals[c] if k[6] == q}
                else:
                    needs = set(arrivals[2])
                if chunk_before is not None:
                    needs.add(("project",) + chunk_before)
                cost = COSTS["select"] if c < 2 else COSTS["fetch"]
                tasks[("select", p, q, c)] = (None, cost, needs)
            tasks[("project", p, q)] = (
                None, COSTS["project"], {("select", p, q, c) for c in range(3)}
            )
            tasks[("x", p, q)] = (("pair", 0), exchange_bytes, {("project", p, q)})
            needs = {("x", p, q)}
            if chunk_before is not None:
                needs.add(("combine",) + chunk_before)
            tasks[("expand", p, q)] = (None, COSTS["expand"], needs)
            tasks[("combine", p, q)] = (None, COSTS["combine"], {("expand", p, q)})
            chunk_before = (p, q)
        tasks[("spread", p)] = (None, COSTS["spread"], set())
        for c, order in enumerate(ORDERS):
            for stage in (2, 1, 0):
                axis = order[stage]
                steps = steps_of(sizes[axis], stage > 0, LONG[c], False)
                for d, s, h in steps:
                    if (d, s - 1, h) in steps:
                        needs = {("r", p, c, stage, d, s - 1, h)}
                    elif stage == 2 and c == 2:
                        needs = {("expand", p, q) for q in range(HALVES)}
                    elif stage == 2:
                        needs = {("combine", p, h)}
                    elif stage == 1 and c == 2:
                        needs = {("spread", p)}
                    else:
                        needs = {
                            k for k in tasks
                            if k[:4] == ("r", p, c, stage + 1)
                            and k[5] == sizes[order[stage + 1]] // 2
                            and (stage == 0 or k[6] == h)
                        }
                    key = ("r", p, c, stage, d, s, h)
                    size = block_bytes(sizes, reduce_widths[c], rows, order, stage, slots)
                    tasks[key] = ((axis, d), size, needs)
                    if c == 2 and stage == 2 and s == sizes[0] // 2:
                        tasks[("spread", p)][2].add(key)
    return tasks


def priority(key):
    if key[0] in "gt":
        return key[1] * 10 + key[3]
    if key[0] == "r":
        return 20 + key[1] * 10 + key[3]
    first = {"pick": -10, "spread": -10, "x": 0, "expand": 10, "combine": 10}
    return key[1] + first.get(key[0], 40)


def schedule(tasks):
    waiting = {k: set(v[2]) for k, v in tasks.items()}
    readers = {}
    for k, v in tasks.items():
        for other in v[2]:
            readers.setdefault(other, []).append(k)
    place = {k: n for n, k in enumerate(tasks)}
    free, pending, arriving, computing, order = {}, {}, [], [], []
    now = 0.0

    def ready(k):
        link = tasks[k][0]
        queue = computing if link is None else pending.setdefault(link, [])
        heapq.heappush(queue, (priority(k), place[k], k))

    def pump():
        for link, queue in pending.items():
            while queue and free.get(link, 0.0) - now < LOOK:
                k = heapq.heappop(queue)[2]
                order.append(("start", k))
                rate = PAIR_RATE if link[0] == "pair" else RATE
                free[link] = max(now, free.get(link, 0.0)) + tasks[k][1] / rate
                heapq.heappush(arriving, (free[link] + LATENCY, place[k], k))

    def finish(k):
        for reader in readers.get(k, ()):
            waiting[reader].discard(k)
            if not waiting[reader]:
                ready(reader)

    for k in tasks:
        if not waiting[k]:
            ready(k)
    pump()
    while arriving or computing:
        if arriving and (arriving[0][0] <= now or not computing):
            when, _, k = heapq.heappop(arriving)
            now = max(now, when) + 0.03
            if k[0] == "r":
                now += tasks[k][1] / ADD_RATE
            order.append(("arrive", k))
        else:
            k = heapq.heappop(computing)[2]
            now += tasks[k][1]
            order.append(("compute", k))
        finish(k)
        pump()
    return order, now


def make_kernel(sizes, widths, rows, experts_here, units):
    nz, nx, ny = sizes
    half_width = sum(widths)
    offsets = (0, widths[0], widths[0] + widths[1])
    gather_widths = (widths[0], widths[1], widths[2] + LANES)
    per_chunk = nz // HALVES
    spe = CAPACITY * nx * ny
    slots = experts_here * spe
    chunk_rows = per_chunk * spe
    group_tokens = nx * ny * rows
    exchange_bytes = experts_here * 2 * chunk_rows * units * 2
    tasks = build_tasks(sizes, gather_widths, widths, rows, exchange_bytes, slots)
    order, _ = schedule(tasks)
    gathers = [k for k in tasks if k[0] in "gt"]
    reduces = [k for k in tasks if k[0] == "r"]
    number = {k: n for n, k in enumerate(gathers)}
    number.update({k: n for n, k in enumerate(reduces)})
    buffers, buffer_of = {}, {}
    for k in reduces:
        p, c, stage = k[1:4]
        first = ORDERS[c][0]
        shape = []
        for a in sorted(ORDERS[c][:stage]):
            shape.append(sizes[a] // 2 if a == first else sizes[a])
        count = buffers.get((p, c, stage), (0,))[0]
        buffer_of[k] = count
        if c == 2 and stage == 2:
            buffers[(p, c, stage)] = (count + 1, slots // 2, widths[c])
        else:
            buffers[(p, c, stage)] = (count + 1,) + tuple(shape) + (rows, widths[c])
    buffer_keys = sorted(buffers)

    def kernel(
        ids_ref, weight_ref, x_ref, lane_hbm, code_hbm, code_t_hbm, gate_hbm, up_hbm, down_hbm,
        out_ref, held01, plane, slotted, tables, table_ref, lane_ref, code_ref, code_t_ref, gate_up, down, chosen,
        outs, pre_out, pre_in, fin_in,
        *rest,
    ):
        landing = dict(zip(buffer_keys, rest[: len(buffer_keys)]))
        (constant_sem, own_sem, pair_send, pair_recv, load_sem, load_send, load_recv,
         gather_send, gather_recv, reduce_send, reduce_recv,
         pre_send, pre_recv, fin_send, fin_recv) = rest[len(buffer_keys):]
        z = lax.axis_index("rep")
        e = lax.axis_index("exp")
        core = lax.rem(e, 2)
        chip = lax.div(e, 2)
        y = lax.rem(chip, ny)
        x = lax.div(chip, ny)
        here = (z, x, y)
        partner = (z, e + 1 - 2 * core)

        def neighbour(axis, direction):
            moved = list(here)
            moved[axis] = lax.rem(here[axis] + direction + sizes[axis], sizes[axis])
            return (moved[0], (moved[1] * ny + moved[2]) * 2 + core)

        def contract_last(a, b):
            return lax.dot_general(
                a, b, (((1,), (1,)), ((), ())), preferred_element_type=jnp.float32
            )

        barrier = pltpu.get_barrier_semaphore()
        peers = [partner] + [neighbour(a, d) for a in range(3) for d in (1, -1)]
        for peer in peers:
            pl.semaphore_signal(barrier, inc=1, device_id=peer, device_id_type=MESH)

        constants = [
            pltpu.make_async_copy(a, b, constant_sem.at[n])
            for n, (a, b) in enumerate(
                ((lane_hbm, lane_ref), (code_hbm, code_ref), (code_t_hbm, code_t_ref))
            )
        ]
        for copy in constants:
            copy.start()

        experts = LANES // 2
        lane = lax.broadcasted_iota(jnp.int32, (rows, LANES), 1)
        named = jnp.zeros((rows, LANES), jnp.float32)
        weights = jnp.zeros((rows, LANES), jnp.float32)
        below = lax.broadcasted_iota(jnp.int32, (rows, rows), 0)
        across = lax.broadcasted_iota(jnp.int32, (rows, rows), 1)
        same = (across == below).astype(jnp.float32).astype(jnp.bfloat16)
        flipped = [
            contract_last(same, ref[...].astype(jnp.float32).astype(jnp.bfloat16))
            for ref in (ids_ref, weight_ref)
        ]
        for k in range(ids_ref.shape[0]):
            name = flipped[0][:, k:k + 1].astype(jnp.int32)
            named = named + (lane == name).astype(jnp.float32)
            weights = weights + jnp.where(lane == name + experts, flipped[1][:, k:k + 1], 0.0)
        triangle = (across <= below).astype(jnp.bfloat16)
        rank = jnp.dot(triangle, named.astype(jnp.bfloat16), preferred_element_type=jnp.float32)
        table_ref[...] = (named * rank + weights).astype(jnp.bfloat16)

        pl.semaphore_wait(barrier, len(peers))

        def pieces(phase):
            mine = (z, x, y, pl.ds(0, rows))
            return (
                (offsets[0], widths[0], held01.at[(0, phase) + mine + (pl.ds(0, widths[0]),)]),
                (offsets[1], widths[1], held01.at[(1, phase) + mine + (pl.ds(0, widths[1]),)]),
                (offsets[2], widths[2], plane.at[phase, x, y, pl.ds(0, rows), pl.ds(0, widths[2])]),
            )

        table_place = plane.at[core, x, y, pl.ds(0, rows), pl.ds(widths[2], LANES)]
        own_copies, pair_copies = [], []
        for n, (column, width, place) in enumerate(pieces(core)):
            start = pl.multiple_of(core * half_width + column, LANES)
            other = pl.multiple_of((1 - core) * half_width + column, LANES)
            own_copies.append((x_ref.at[:, pl.ds(start, width)], place))
            pair_copies.append((x_ref.at[:, pl.ds(other, width)], place))
        own_copies.append((table_ref, table_place))
        pair_copies.append((table_ref, table_place))
        own_copies = [
            pltpu.make_async_copy(a, b, own_sem.at[n]) for n, (a, b) in enumerate(own_copies)
        ]
        pair_copies = [
            pltpu.make_async_remote_copy(
                src_ref=a, dst_ref=b, send_sem=pair_send.at[n], recv_sem=pair_recv.at[n],
                device_id=partner, device_id_type=MESH,
            )
            for n, (a, b) in enumerate(pair_copies)
        ]
        for copy in pair_copies + own_copies:
            copy.start()

        local = experts_here // 2
        mine_experts = pl.ds(core * local, local)
        loads, sends = [], []
        for n, (source, target) in enumerate(
            (
                (gate_hbm, gate_up.at[mine_experts, 0]),
                (up_hbm, gate_up.at[mine_experts, 1]),
                (down_hbm, down.at[mine_experts]),
            )
        ):
            start = pl.multiple_of(core * half_width, LANES)
            other = pl.multiple_of((1 - core) * half_width, LANES)
            loads.append(
                pltpu.make_async_copy(
                    source.at[:, :, pl.ds(start, half_width)], target, load_sem.at[n]
                )
            )
            sends.append(
                pltpu.make_async_remote_copy(
                    src_ref=source.at[:, :, pl.ds(other, half_width)], dst_ref=target,
                    send_sem=load_send.at[n], recv_sem=load_recv.at[n], device_id=partner,
                    device_id_type=MESH,
                )
            )
        for copy in own_copies + pair_copies:
            copy.wait()
        for copy in loads + sends:
            copy.start()

        def block(p, c, stage, index, half, width):
            if c == 3:
                return tables.at[p, index]
            if c == 2 and stage == 2:
                part = slots // 2
                return slotted.at[p, index, pl.ds(half * part, part)]
            axes = ORDERS[c]
            where = []
            for a in range(3):
                if a == axes[stage]:
                    where.append(index)
                elif a in axes[:stage]:
                    if a == axes[0]:
                        where.append(pl.ds(half * (sizes[a] // 2), sizes[a] // 2))
                    else:
                        where.append(pl.ds(0, sizes[a]))
                else:
                    where.append(here[a])
            if c == 2:
                return plane.at[(p,) + tuple(where[1:]) + (pl.ds(0, rows), pl.ds(0, width))]
            return held01.at[(c, p) + tuple(where) + (pl.ds(0, rows), pl.ds(0, width))]

        def gather_copy(key, received):
            _, p, c, stage, d, s, h = key
            axis = ORDERS[c][stage] if c < 3 else 0
            back = s if received else s - 1
            index = lax.rem(here[axis] - d * back + sizes[axis], sizes[axis])
            place = block(p, c, stage, index, h, gather_widths[c] if c < 3 else LANES)
            n = number[key]
            return pltpu.make_async_remote_copy(
                src_ref=place, dst_ref=place, send_sem=gather_send.at[n],
                recv_sem=gather_recv.at[n], device_id=neighbour(axis, d), device_id_type=MESH,
            )

        def reduce_copy(key):
            _, p, c, stage, d, s, h = key
            axis = ORDERS[c][stage]
            size = sizes[axis]
            index = lax.rem(here[axis] + d * (size // 2 - s + 1) + size, size)
            n = number[key]
            return pltpu.make_async_remote_copy(
                src_ref=block(p, c, stage, index, h, widths[c]),
                dst_ref=landing[(p, c, stage)].at[buffer_of[key]],
                send_sem=reduce_send.at[n], recv_sem=reduce_recv.at[n],
                device_id=neighbour(axis, d), device_id_type=MESH,
            )

        def pre_copy(p, q):
            n = p * HALVES + q
            return pltpu.make_async_remote_copy(
                src_ref=pre_out.at[n], dst_ref=pre_in.at[n], send_sem=pre_send.at[n],
                recv_sem=pre_recv.at[n], device_id=partner, device_id_type=MESH,
            )

        base = chip * experts_here

        def table_of(p, gz):
            return tables[p, gz].reshape(group_tokens, LANES)

        def onehot_of(table):
            wanted = (lane_ref[...] == base).astype(jnp.bfloat16)
            return (contract_last(wanted, table) == code_ref[...]).astype(jnp.bfloat16)

        def scatter_of(table):
            wanted = (lane_ref[...] == base).astype(jnp.bfloat16)
            weigh = (lane_ref[...] == base + experts).astype(jnp.bfloat16)
            codes = contract_last(table, wanted)
            values = contract_last(table, weigh)
            return jnp.where(codes == code_t_ref[...], values, 0.0).astype(jnp.bfloat16)

        def pick_rows(p):
            tables[p, z] = plane[p, :, :, :, pl.ds(widths[2], LANES)]
            value = plane[p, :, :, :, pl.ds(0, widths[2])].reshape(group_tokens, widths[2])
            slotted[p, z] = jnp.dot(
                onehot_of(table_of(p, z)), value, preferred_element_type=jnp.float32
            ).astype(jnp.bfloat16)

        def spread(p):
            plane[p, :, :, :, pl.ds(0, widths[2])] = jnp.dot(
                scatter_of(table_of(p, z)), slotted[p, z], preferred_element_type=jnp.float32
            ).astype(jnp.bfloat16).reshape(nx, ny, rows, widths[2])

        def select(p, q, c):
            columns = pl.ds(offsets[c], widths[c])

            def one(g, carry):
                gz = q * per_chunk + g
                if c == 2:
                    picked = slotted[p, gz]
                else:
                    value = held01[c, p, gz].reshape(group_tokens, widths[c])
                    picked = jnp.dot(
                        onehot_of(table_of(p, gz)), value, preferred_element_type=jnp.float32
                    ).astype(jnp.bfloat16)
                for n in range(experts_here):
                    chosen[n, pl.ds(pl.multiple_of(g * spe, 16), spe), columns] = (
                        picked[n * spe:(n + 1) * spe]
                    )
                return carry

            lax.fori_loop(0, per_chunk, one, 0)

        def project(p, q):
            def one(n, carry):
                for which in range(2):
                    pre_out[p * HALVES + q, n, which] = contract_last(
                        chosen[n], gate_up[n, which]
                    ).astype(jnp.bfloat16)
                return carry

            lax.fori_loop(0, experts_here, one, 0)

        def expand(p, q):
            index = p * HALVES + q

            def one(n, carry):
                values = []
                for which in range(2):
                    mine = pre_out[index, n, which].astype(jnp.float32)
                    values.append(mine + pre_in[index, n, which].astype(jnp.float32))
                hidden = values[0] / (1.0 + jnp.exp(-values[0])) * values[1]
                outcome = jnp.dot(
                    hidden.astype(jnp.bfloat16), down[n], preferred_element_type=jnp.float32
                ).astype(jnp.bfloat16)
                for g in range(per_chunk):
                    place = pl.ds(pl.multiple_of(n * spe, 16), spe)
                    part = outcome[g * spe:(g + 1) * spe]
                    outs[g, place] = part[:, :offsets[2]]
                    slotted[p, q * per_chunk + g, place] = part[:, offsets[2]:]
                return carry

            lax.fori_loop(0, experts_here, one, 0)

        def combine(p, q):
            def one(g, carry):
                gz = q * per_chunk + g
                scatter = scatter_of(table_of(p, gz))
                for c in range(2):
                    held01[c, p, gz] = jnp.dot(
                        scatter, outs[g, :, pl.ds(offsets[c], widths[c])],
                        preferred_element_type=jnp.float32,
                    ).astype(jnp.bfloat16).reshape(nx, ny, rows, widths[c])
                return carry

            lax.fori_loop(0, per_chunk, one, 0)

        def add_into(target, sources):
            lead = target.shape[:-2]

            def one_block(where):
                total = target[where].astype(jnp.float32)
                for source in sources:
                    total = total + source[where].astype(jnp.float32)
                target[where] = total.astype(jnp.bfloat16)

            if not lead:
                one_block(...)
                return

            def one(n, carry):
                if len(lead) == 1:
                    one_block((n,))
                else:
                    for m in range(lead[1]):
                        one_block((n, m))
                return carry

            lax.fori_loop(0, lead[0], one, 0)

        arrived = set()

        def reduce_arrival(key):
            reduce_copy(key).wait_recv()
            arrived.add(key)
            _, p, c, stage, d, s, h = key
            axis = ORDERS[c][stage]
            size = sizes[axis]
            last = size // 2
            width = widths[c]
            if s < last:
                index = lax.rem(here[axis] + d * (last - s) + size, size)
                add_into(
                    block(p, c, stage, index, h, width),
                    [landing[(p, c, stage)].at[buffer_of[key]]],
                )
                return
            parts = [k for k in reduces if k[:4] == key[:4] and k[5] == last and k[6] == h]
            if all(k in arrived for k in parts):
                add_into(
                    block(p, c, stage, here[axis], h, width),
                    [landing[(p, c, stage)].at[buffer_of[k]] for k in parts],
                )

        loaded = set()
        for kind, key in order:
            if kind == "start":
                if key[0] in "gt":
                    gather_copy(key, False).start()
                elif key[0] == "r":
                    reduce_copy(key).start()
                else:
                    pre_copy(key[1], key[2]).start()
            elif kind == "arrive":
                if key[0] in "gt":
                    gather_copy(key, True).wait_recv()
                elif key[0] == "r":
                    reduce_arrival(key)
                else:
                    pre_copy(key[1], key[2]).wait_recv()
            elif key[0] == "pick":
                if "constants" not in loaded:
                    loaded.add("constants")
                    for copy in constants:
                        copy.wait()
                pick_rows(key[1])
            elif key[0] == "spread":
                spread(key[1])
            elif key[0] == "select":
                select(*key[1:])
            elif key[0] == "project":
                if "weights" not in loaded:
                    loaded.add("weights")
                    for copy in loads + sends:
                        copy.wait()
                project(*key[1:])
            elif key[0] == "expand":
                if key[2] == 0:
                    for k in gathers:
                        if k[1] == key[1]:
                            gather_copy(k, False).wait_send()
                expand(*key[1:])
            else:
                combine(*key[1:])

        last_copies = [
            pltpu.make_async_remote_copy(
                src_ref=place, dst_ref=fin_in.at[:, pl.ds(column, width)], send_sem=fin_send.at[n],
                recv_sem=fin_recv.at[n], device_id=partner, device_id_type=MESH,
            )
            for n, (column, width, place) in enumerate(pieces(1 - core))
        ]
        for copy in last_copies:
            copy.start()
        for column, width, place in pieces(core):
            start = pl.multiple_of(core * half_width + column, LANES)
            out_ref[:, pl.ds(start, width)] = place[...]
        for k in reduces:
            reduce_copy(k).wait_send()
        for p in range(PHASES):
            for q in range(HALVES):
                pre_copy(p, q).wait_send()
        for copy in last_copies:
            copy.wait()
        out_ref[:, pl.ds(pl.multiple_of((1 - core) * half_width, LANES), half_width)] = fin_in[...]

    bf16 = jnp.bfloat16
    dma = pltpu.SemaphoreType.DMA
    chunks = PHASES * HALVES
    pre_shape = (chunks, experts_here, 2, chunk_rows, units)
    scratch = [
        pltpu.VMEM((2, PHASES, nz, nx, ny, rows, widths[0]), bf16),
        pltpu.VMEM((PHASES, nx, ny, rows, widths[2] + LANES), bf16),
        pltpu.VMEM((PHASES, nz, slots, widths[2]), bf16),
        pltpu.VMEM((PHASES, nz, nx, ny, rows, LANES), bf16),
        pltpu.VMEM((rows, LANES), bf16),
        pltpu.VMEM((slots, LANES), jnp.int32),
        pltpu.VMEM((slots, group_tokens), jnp.float32),
        pltpu.VMEM((group_tokens, slots), jnp.float32),
        pltpu.VMEM((experts_here, 2, units, half_width), bf16),
        pltpu.VMEM((experts_here, units, half_width), bf16),
        pltpu.VMEM((experts_here, chunk_rows, half_width), bf16),
        pltpu.VMEM((per_chunk, slots, offsets[2]), bf16),
        pltpu.VMEM(pre_shape, bf16),
        pltpu.VMEM(pre_shape, bf16),
        pltpu.VMEM((rows, half_width), bf16),
        *[pltpu.VMEM(buffers[k], bf16) for k in buffer_keys],
        dma((3,)), dma((4,)), dma((4,)), dma((4,)), dma((3,)), dma((3,)), dma((3,)),
        dma((len(gathers),)), dma((len(gathers),)), dma((len(reduces),)), dma((len(reduces),)),
        dma((chunks,)), dma((chunks,)), dma((3,)), dma((3,)),
    ]
    slot = np.arange(slots)
    token = np.arange(group_tokens)
    lane_constant = (np.arange(LANES)[None, :] - (slot // spe)[:, None]).astype(np.int32)
    same = (slot % spe // CAPACITY)[:, None] == (token // rows)[None, :]
    code = np.where(same, (slot % CAPACITY + 1)[:, None], -1).astype(np.float32)
    return kernel, scratch, (lane_constant, code, np.ascontiguousarray(code.T))


def solution(mesh):
    nz = mesh.shape["rep"]
    nx = int(round((mesh.shape["exp"] // 2) ** 0.5))
    ny = mesh.shape["exp"] // 2 // nx

    def on_device(tokens, routed_experts, route_weights, gate_weight, up_weight, down_weight):
        rows, width = tokens.shape
        local, units = gate_weight.shape[:2]
        thin = max(1, 5 * (width // 2 // LANES) // 16) * LANES
        widths = (thin, thin, width // 2 - 2 * thin)
        kernel, scratch, constants = make_kernel((nz, nx, ny), widths, rows, 2 * local, units)
        vmem = pl.BlockSpec(memory_space=pltpu.VMEM)
        hbm = pl.BlockSpec(memory_space=pl.ANY)
        return pl.pallas_call(
            kernel,
            out_shape=jax.ShapeDtypeStruct((rows, width), jnp.bfloat16),
            in_specs=[vmem] * 2 + [hbm] * 7,
            out_specs=vmem,
            scratch_shapes=scratch,
            compiler_params=pltpu.CompilerParams(
                collective_id=0, has_side_effects=True, vmem_limit_bytes=67_000_000
            ),
        )(
            routed_experts.T, route_weights.T, tokens, *constants, gate_weight, up_weight,
            down_weight,
        )

    placed = (
        P(("rep", "exp"), None),
        P(("rep", "exp"), None),
        P(("rep", "exp"), None),
        P("exp", "rep", None),
        P("exp", "rep", None),
        P("exp", "rep", None),
    )
    return jax.shard_map(
        on_device, mesh=mesh, in_specs=placed, out_specs=P(("rep", "exp"), None), check_vma=False
    )
```
